256 devices in a mesh: blk: 64 (over x_hi, y, z), row: 4 (over x_lo, core).
Axes of the slice: x: 4 (x_hi: 2, x_lo: 2; x = x_hi * 2 + x_lo), y: 4, z: 8, core: 2. Of those that a mesh axis runs over, the one named last changes fastest.
Arguments:
- pool_embeds: bfloat16 [65536, 768], P('blk'), may hold values from -24 to 24
- target_samples: bfloat16 [16384, 768], P(('blk', 'row')), may hold values from -6 to 6
- reference_samples: bfloat16 [16384, 768], P(('blk', 'row')), may hold values from -6 to 6
Outputs:
- log_ratio: float32 [65536], P('blk')
- standardized: float32 [65536], P('blk')
The draws below stay inside these ranges and needn't reach their ends.
All inputs are finite; a program needn't handle non-finite values.
Results may differ from the reference program's by a relative error of at most 0.0003.
Values may be sent and summed in bfloat16 or wider, within the bound.
No kernel may reach another device: no remote copies, remote signals or barrier semaphores. Data moves between devices by JAX's collectives and lax.ppermute only.
A program may use at most 128 MiB of HBM per device.

```python
import jax
import jax.numpy as jnp
from jax import lax

D = 768
NPOOL = 65536
NSAMP = 16384


def sample_set(key, set_index):
    local_key = jax.random.fold_in(key, 101 + set_index)
    normal_key, pick_key, extra_key = jax.random.split(local_key, 3)
    spread_scale = 1.0 + 0.15 * set_index
    pick_draw = jax.random.randint(pick_key, (NSAMP,), 0, 32)
    forced = jax.random.randint(extra_key, (), 0, NSAMP)
    chosen = (pick_draw == 0) | (jnp.arange(NSAMP, dtype=jnp.int32) == forced)
    factor = jnp.where(chosen, 2.2, 1.0).astype(jnp.float32)
    raw_values = jax.random.normal(normal_key, (NSAMP, D), jnp.float32)
    values = jnp.clip(raw_values * spread_scale * factor[:, None], -6.0, 6.0)
    return (values, chosen)


def copy_rows(samples, chosen, row_picks):
    flags = 1 - chosen.astype(jnp.int32)
    sorted_rows = jnp.argsort(flags, stable=True)
    chosen_count = jnp.maximum(jnp.sum(chosen.astype(jnp.int32)), 1)
    return samples[sorted_rows[row_picks % chosen_count]]


def draw_target_samples(key, part):
    values, chosen = sample_set(key, 0)
    return values.astype(jnp.bfloat16)


def draw_reference_samples(key, part):
    values, chosen = sample_set(key, 1)
    return values.astype(jnp.bfloat16)


def draw_pool_embeds(key, part):
    first_key, second_key = jax.random.split(key)
    kind_key = jax.random.fold_in(key, 201)
    choose_key = jax.random.fold_in(key, 202)
    noise_key = jax.random.fold_in(key, 203)
    base = jnp.clip(jax.random.normal(first_key, (NPOOL, D), jnp.float32), -6.0, 6.0)
    position = jnp.arange(NPOOL, dtype=jnp.float32) / NPOOL
    row_scale = jax.random.uniform(second_key, (NPOOL, 1), jnp.float32, 0.6, 1.4)
    base_rows = base * row_scale * (0.7 + 0.6 * position[:, None])
    target_set, target_chosen = sample_set(key, 0)
    ref_set, ref_chosen = sample_set(key, 1)
    row_kind = jax.random.randint(kind_key, (NPOOL,), 0, 64)
    row_picks = jax.random.randint(choose_key, (NPOOL,), 0, 1 << 20)
    near_target = copy_rows(target_set, target_chosen, row_picks)
    near_ref = copy_rows(ref_set, ref_chosen, row_picks)
    noise = 0.3 * jnp.clip(jax.random.normal(noise_key, (NPOOL, D), jnp.float32), -6.0, 6.0)
    mixed = jnp.where(row_kind[:, None] == 0, near_target + noise, jnp.where(row_kind[:, None] == 1, near_ref + noise, base_rows))
    return mixed.astype(jnp.bfloat16)


def setup_inputs(seed: int = 0) -> dict:
    splits = jax.random.split(jax.random.key(seed), 4)
    pool_embeds = draw_pool_embeds(jax.random.fold_in(splits[3], 71), 0)
    target_samples = draw_target_samples(jax.random.fold_in(splits[3], 71), 0)
    reference_samples = draw_reference_samples(jax.random.fold_in(splits[3], 71), 0)
    return dict(pool_embeds=pool_embeds, target_samples=target_samples, reference_samples=reference_samples)


KERNEL_GAIN = 30.0

def log_density(pool_rows, samples, sample_norms):
    pool_norms = lax.optimization_barrier(jnp.sum(jnp.square(pool_rows.astype(jnp.float32)), axis=1))
    products = jnp.dot(pool_rows, samples.T, preferred_element_type=jnp.float32)
    scores = (2.0 * products - pool_norms[:, None] - sample_norms[None, :]) * (KERNEL_GAIN / D)
    return jax.nn.logsumexp(scores, axis=1)

def reference(pool_embeds, target_samples, reference_samples):
    target_norms = lax.optimization_barrier(jnp.sum(jnp.square(target_samples.astype(jnp.float32)), axis=1))
    ref_norms = lax.optimization_barrier(jnp.sum(jnp.square(reference_samples.astype(jnp.float32)), axis=1))
    blocked = pool_embeds.reshape(NPOOL // 256, 256, D)

    def per_block(pool_rows):
        return log_density(pool_rows, target_samples, target_norms) - log_density(pool_rows, reference_samples, ref_norms)
    log_ratio = lax.map(per_block, blocked).reshape(NPOOL)
    mean_value = jnp.sum(log_ratio) / NPOOL
    variance = jnp.sum(jnp.square(log_ratio - mean_value)) / NPOOL
    standardized = (log_ratio - mean_value) / jnp.sqrt(variance + 1e-05)
    return (log_ratio, standardized)
```

```python
import functools

import jax
import jax.numpy as jnp
from jax import lax
from jax.experimental import pallas as pl
from jax.experimental.pallas import tpu as pltpu
from jax.sharding import Mesh, PartitionSpec as P

KERNEL_GAIN = 30.0
TILE = 256
SIZES = {"xh": 2, "y": 4, "z": 8, "xl": 2, "core": 2}
ROW_GROUP = ("y", "xl", "core")
BLK = ("xh", "y", "z")


def partial_kernel(n_pool, n_samples, scale, *refs):
    pools = refs[:n_pool]
    samples = refs[n_pool : n_pool + n_samples]
    out_ref = refs[n_pool + n_samples]
    joined, half_norm, buf0, buf1 = refs[n_pool + n_samples + 1 :]
    rows = joined.shape[0]
    member = rows // 2
    each = samples[0].shape[0] // 2
    for i, ref in enumerate(samples):
        joined[i * each : (i + 1) * each, :] = ref[:each, :]
        joined[member + i * each : member + (i + 1) * each, :] = ref[each:, :]
    step = 128
    for r in range(0, rows, step):
        wide = joined[r : r + step, :].astype(jnp.float32)
        norm = jnp.sum(wide * wide, axis=1, keepdims=True) * 0.5
        half_norm[r : r + step, :] = jnp.broadcast_to(norm, (step, 128))

    def product(pool, tile, buf):
        start = pl.multiple_of(tile * TILE, TILE)
        weights = pool[pl.ds(start, TILE), :]
        buf[...] = lax.dot_general(
            joined[...], weights, (((1,), (1,)), ((), ())), preferred_element_type=jnp.float32
        )

    def finish(buf, column):
        column = pl.multiple_of(column, TILE)
        for m in range(2):
            for c in range(0, TILE, 128):
                rows_of = slice(m * member, (m + 1) * member)
                values = buf[rows_of, c : c + 128] - half_norm[rows_of, :]
                high = jnp.max(values, axis=0, keepdims=True)
                total = jnp.sum(jnp.exp((values - high) * scale), axis=0, keepdims=True)
                out_ref[m : m + 1, pl.ds(column + c, 128)] = high * scale + jnp.log(total)

    offset = 0
    for pool in pools:
        tiles = pool.shape[0] // TILE
        product(pool, 0, buf0)

        def pair(i, _, pool=pool, offset=offset, tiles=tiles):
            product(pool, 2 * i + 1, buf1)
            finish(buf0, offset + 2 * i * TILE)
            product(pool, jnp.minimum(2 * i + 2, tiles - 1), buf0)
            finish(buf1, offset + (2 * i + 1) * TILE)
            return 0

        lax.fori_loop(0, tiles // 2, pair, 0)
        offset += pool.shape[0]


def partial_lse(pools, samples, scale):
    count = sum(p.shape[0] for p in pools)
    rows = sum(s.shape[0] for s in samples)
    depth = pools[0].shape[1]
    return pl.pallas_call(
        functools.partial(partial_kernel, len(pools), len(samples), scale),
        out_shape=jax.ShapeDtypeStruct((2, count), jnp.float32),
        in_specs=[pl.BlockSpec(memory_space=pltpu.VMEM)] * (len(pools) + len(samples)),
        out_specs=pl.BlockSpec(memory_space=pltpu.VMEM),
        scratch_shapes=[
            pltpu.VMEM((rows, depth), jnp.bfloat16),
            pltpu.VMEM((rows, 128), jnp.float32),
            pltpu.VMEM((rows, TILE), jnp.float32),
            pltpu.VMEM((rows, TILE), jnp.float32),
        ],
        compiler_params=pltpu.CompilerParams(vmem_limit_bytes=32 * 1024 * 1024),
        cost_estimate=pl.CostEstimate(
            flops=2 * rows * count * depth, bytes_accessed=2 * (rows + count) * depth, transcendentals=rows * count
        ),
    )(*pools, *samples)


def shift(value, axis, by):
    n = SIZES[axis]
    return lax.ppermute(value, axis, [(i, (i + by) % n) for i in range(n)])


def swap_core(value):
    return lax.ppermute(value, "core", [(0, 1), (1, 0)])


def body(pool_embeds, target_samples, reference_samples):
    count, depth = pool_embeds.shape
    half = count // 2
    core = lax.axis_index("core")
    scale = 2.0 * KERNEL_GAIN / depth

    own = jnp.concatenate([target_samples, reference_samples], axis=0)
    other = lax.ppermute(own, ("xh", "xl"), [(0, 3), (3, 0), (1, 2), (2, 1)])
    mine = lax.dynamic_slice_in_dim(pool_embeds, core * half, half, 0)
    from_left = shift(mine, "y", 1)
    from_right = shift(mine, "y", -1)
    samples = [own, other]
    for start in (own, other):
        up, down = start, start
        for _ in range(3):
            up, down = shift(up, "z", 1), shift(down, "z", -1)
            samples += [up, down]
        width = own.shape[0] // 4
        parts_up = jnp.concatenate([up[:width], up[2 * width : 3 * width]], axis=0)
        parts_down = jnp.concatenate([down[width : 2 * width], down[3 * width :]], axis=0)
        samples += [shift(parts_up, "z", 1), shift(parts_down, "z", -1)]
    full = [s for s in samples if s.shape[0] == own.shape[0]]
    halves = [s for s in samples if s.shape[0] != own.shape[0]]
    for a, b in zip(halves[0::2], halves[1::2]):
        w = own.shape[0] // 4
        full.append(jnp.concatenate([a[:w], b[:w], a[w:], b[w:]], axis=0))
    quarter = half // 2
    across = jnp.concatenate([shift(from_left[:quarter], "y", 1), shift(from_right[quarter:], "y", -1)], axis=0)
    pools = [pool_embeds, from_left, swap_core(from_left), across, swap_core(across), from_right, swap_core(from_right)]
    lse = partial_lse(pools, full, scale)

    pieces = lse.reshape(2, 4, count).transpose(1, 0, 2)
    y = lax.axis_index("y")
    by_owner = jnp.take(pieces, (y - jnp.arange(4)) % 4, axis=0)
    send = jnp.broadcast_to(by_owner[:, None], (4, 4, 2, count)).reshape(16, 2, count)
    got = lax.all_to_all(send, ROW_GROUP, 0, 0).reshape(4, 2, 2, 2, 2, half)
    flipped = got[..., ::-1, :]
    sender_y = jnp.arange(4).reshape(4, 1, 1, 1, 1, 1)
    sender_core = jnp.arange(2).reshape(1, 1, 2, 1, 1, 1)
    got = jnp.where((sender_y != y) & (sender_core == 1), flipped, got).reshape(16, 2, count)
    high = jnp.max(got, axis=0)
    joined = high + jnp.log(jnp.sum(jnp.exp(got - high), axis=0))
    pool_norms = jnp.sum(jnp.square(pool_embeds.astype(jnp.float32)), axis=1) * (KERNEL_GAIN / depth)
    log_target = joined[0] - pool_norms
    log_ref = joined[1] - pool_norms
    log_ratio = log_target - log_ref

    block_mean = jnp.sum(log_ratio) / count
    block_square = jnp.sum(jnp.square(log_ratio - block_mean)) / count
    lane = lax.broadcasted_iota(jnp.int32, (64, 128), 1)
    stats = jnp.where(lane == 0, block_mean, jnp.where(lane == 1, block_square, 0.0))
    stats = lax.all_to_all(stats, BLK, 0, 0, tiled=True)
    mean_value = jnp.sum(stats[:, 0]) / 64
    variance = jnp.sum(stats[:, 1] + jnp.square(stats[:, 0] - mean_value)) / 64
    standardized = (log_ratio - mean_value) / jnp.sqrt(variance + 1e-05)
    return (log_ratio, standardized)


def solution(mesh):
    fine = Mesh(mesh.devices.reshape(2, 4, 8, 2, 2), ("xh", "y", "z", "xl", "core"))
    rows = P(BLK, None)
    samples = P(("xh", "y", "z", "xl", "core"), None)
    return jax.shard_map(
        body, mesh=fine, in_specs=(rows, samples, samples), out_specs=(P(BLK), P(BLK)), check_vma=False
    )
```

```python
import functools

import jax
import jax.numpy as jnp
from jax import lax
from jax.experimental import pallas as pl
from jax.experimental.pallas import tpu as pltpu
from jax.sharding import Mesh, PartitionSpec as P

KERNEL_GAIN = 30.0
TILE = 256
CHUNK = 256
SIZES = {"xh": 2, "y": 4, "z": 8, "xl": 2, "core": 2}
ROW_GROUP = ("y", "xl", "core")
BLK = ("xh", "y", "z")
VMEM = pl.BlockSpec(memory_space=pltpu.VMEM)


def lse_tiles(pools, samples, scale, out_ref, joined, half_norm, pool_all, bufs, tops):
    rows = joined.shape[0]
    member = rows // 2
    each = samples[0].shape[0] // 2
    for i, ref in enumerate(samples):
        joined[i * each : (i + 1) * each, :] = ref[:each, :]
        joined[member + i * each : member + (i + 1) * each, :] = ref[each:, :]
    count = 0
    for ref in pools:
        pool_all[count : count + ref.shape[0], :] = ref[...]
        count += ref.shape[0]

    def norms(i, _):
        at = pl.ds(pl.multiple_of(i * 128, 128), 128)
        wide = joined[at, :].astype(jnp.float32)
        half_norm[at, :] = jnp.broadcast_to(jnp.sum(wide * wide, axis=1, keepdims=True) * 0.5, (128, 128))
        return 0

    lax.fori_loop(0, rows // 128, norms, 0)
    tiles = count // TILE

    def step(tile, buf, top, done, done_buf, done_top):
        if tile is not None:
            weights = pool_all[pl.ds(pl.multiple_of(tile * TILE, TILE), TILE), :]
        if done is not None:
            high = [jnp.max(done_top[8 * m : 8 * m + 8, :], axis=0, keepdims=True) for m in range(2)]
        highs, totals = [None, None], [None, None]
        for c in range(rows // CHUNK):
            m = c * CHUNK // member
            at = slice(c * CHUNK, (c + 1) * CHUNK)
            if tile is not None:
                products = lax.dot_general(
                    joined[at, :], weights, (((1,), (1,)), ((), ())), preferred_element_type=jnp.float32
                )
                values = products - jnp.concatenate([half_norm[at, :]] * (TILE // 128), axis=1)
                buf[at, :] = values
                top_of = jnp.max(values.reshape(CHUNK // 8, 8, TILE), axis=0)
                highs[m] = top_of if highs[m] is None else jnp.maximum(highs[m], top_of)
            if done is not None:
                powers = jnp.exp((done_buf[at, :] - high[m]) * scale)
                total = jnp.sum(powers.reshape(CHUNK // 8, 8, TILE), axis=0)
                totals[m] = total if totals[m] is None else totals[m] + total
        if tile is not None:
            for m in range(2):
                top[8 * m : 8 * m + 8, :] = highs[m]
        if done is not None:
            for m in range(2):
                value = high[m] * scale + jnp.log(jnp.sum(totals[m], axis=0, keepdims=True))
                for k in range(TILE // 128):
                    out_ref[m, pl.ds(done * (TILE // 128) + k, 1), :] = value[:, k * 128 : (k + 1) * 128]

    step(0, bufs[0], tops[0], None, None, None)

    def pair(i, _):
        step(2 * i + 1, bufs[1], tops[1], 2 * i, bufs[0], tops[0])
        step(2 * i + 2, bufs[0], tops[0], 2 * i + 1, bufs[1], tops[1])
        return 0

    lax.fori_loop(0, tiles // 2 - 1, pair, 0)
    step(tiles - 1, bufs[1], tops[1], tiles - 2, bufs[0], tops[0])
    step(None, None, None, tiles - 1, bufs[1], tops[1])


def partial_kernel(n_pools, n_samples, scale, *refs):
    pools, samples, out_ref = refs[:n_pools], refs[n_pools : n_pools + n_samples], refs[n_pools + n_samples]
    joined, half_norm, pool_all, buf0, buf1, top0, top1 = refs[n_pools + n_samples + 1 :]
    lse_tiles(pools, samples, scale, out_ref, joined, half_norm, pool_all, (buf0, buf1), (top0, top1))


def add_exp(a, b):
    high = jnp.maximum(a, b)
    return high + jnp.log(jnp.exp(a - high) + jnp.exp(b - high))


def last_kernel(n_pools, n_samples, scale, place, *refs):
    pools, samples = refs[:n_pools], refs[n_pools : n_pools + n_samples]
    first, second, out_ref, across = refs[n_pools + n_samples : n_pools + n_samples + 4]
    joined, half_norm, pool_all, buf0, buf1, top0, top1 = refs[n_pools + n_samples + 4 :]
    lse_tiles(pools, samples, scale, across, joined, half_norm, pool_all, (buf0, buf1), (top0, top1))
    y, core = place[0], place[1]
    near = add_exp(first[...], second[...])
    n = near.shape[1] // 3
    far = across[...]

    def put(owner, value, swapped):
        half = n // 2
        for j in range(4):
            at = lax.rem(owner, 4) * 4 + j
            if swapped:
                out_ref[at, :, pl.ds(core * half, half), :] = value[:, :half, :]
                out_ref[at, :, pl.ds((1 - core) * half, half), :] = value[:, half:, :]
            else:
                out_ref[at, :, :, :] = value

    put(y, near[:, :n, :], False)
    put(y + 3, near[:, n : 2 * n, :], True)
    put(y + 1, near[:, 2 * n :, :], True)
    put(y + 2, far, True)


def lse_call(pools, samples, scale, earlier=None, place=None):
    count = sum(p.shape[0] for p in pools)
    rows = sum(s.shape[0] for s in samples)
    depth = pools[0].shape[1]
    scratch = [
        pltpu.VMEM((rows, depth), jnp.bfloat16),
        pltpu.VMEM((rows, 128), jnp.float32),
        pltpu.VMEM((count, depth), jnp.bfloat16),
        pltpu.VMEM((rows, TILE), jnp.float32),
        pltpu.VMEM((rows, TILE), jnp.float32),
        pltpu.VMEM((16, TILE), jnp.float32),
        pltpu.VMEM((16, TILE), jnp.float32),
    ]
    partial = jax.ShapeDtypeStruct((2, count // 128, 128), jnp.float32)
    common = dict(
        out_specs=VMEM,
        compiler_params=pltpu.CompilerParams(vmem_limit_bytes=30 * 1024 * 1024),
        cost_estimate=pl.CostEstimate(
            flops=2 * rows * count * depth, bytes_accessed=2 * (rows + count) * depth, transcendentals=rows * count
        ),
    )
    inputs = [VMEM] * (len(pools) + len(samples))
    if earlier is None:
        kernel = functools.partial(partial_kernel, len(pools), len(samples), scale)
        return pl.pallas_call(kernel, out_shape=partial, in_specs=inputs, scratch_shapes=scratch, **common)(*pools, *samples)
    kernel = functools.partial(last_kernel, len(pools), len(samples), scale)
    return pl.pallas_call(
        kernel,
        out_shape=jax.ShapeDtypeStruct((16,) + partial.shape, jnp.float32),
        in_specs=[pl.BlockSpec(memory_space=pltpu.SMEM)] + inputs + [VMEM] * 2,
        scratch_shapes=[pltpu.VMEM(partial.shape, jnp.float32)] + scratch,
        **common,
    )(place, *pools, *samples, *earlier)


def merge_kernel(got, norms, ratio_ref, stats_ref):
    value = got[...]
    high = jnp.max(value, axis=0)
    total = high + jnp.log(jnp.sum(jnp.exp(value - high[None]), axis=0))
    log_target = total[0] - norms[...]
    log_ref = total[1] - norms[...]
    ratio = log_target - log_ref
    ratio_ref[...] = ratio
    count = ratio.shape[0] * ratio.shape[1]
    mean = jnp.sum(ratio, axis=(0, 1), keepdims=True) / count
    square = jnp.sum(jnp.square(ratio - mean), axis=(0, 1), keepdims=True) / count
    lane = lax.broadcasted_iota(jnp.int32, stats_ref.shape, 1)
    stats_ref[...] = jnp.where(lane == 0, mean, jnp.where(lane == 1, square, 0.0))


def finish_kernel(ratio, stats, out_ref):
    blocks = stats.shape[0]
    value = stats[...]
    mean = jnp.sum(value[:, 0:1], axis=0, keepdims=True) / blocks
    variance = jnp.sum(value[:, 1:2] + jnp.square(value[:, 0:1] - mean), axis=0, keepdims=True) / blocks
    out_ref[...] = (ratio[...] - mean) / jnp.sqrt(variance + 1e-05)


def shift(value, axis, by):
    n = SIZES[axis]
    return lax.ppermute(value, axis, [(i, (i + by) % n) for i in range(n)])


def swap_core(value):
    return lax.ppermute(value, "core", [(0, 1), (1, 0)])


def swap_x(value):
    return lax.ppermute(value, ("xh", "xl"), [(0, 3), (3, 0), (1, 2), (2, 1)])


def body(pool_embeds, target_samples, reference_samples):
    count, depth = pool_embeds.shape
    half = count // 2
    quarter = half // 2
    core = lax.axis_index("core")
    scale = 2.0 * KERNEL_GAIN / depth

    mine = lax.dynamic_slice_in_dim(pool_embeds, core * half, half, 0)
    left, right = shift(mine, "y", 1), shift(mine, "y", -1)
    own = jnp.concatenate([target_samples, reference_samples], axis=0)
    other = swap_x(own)
    up1, down1 = shift(own, "z", 1), shift(own, "z", -1)
    other_up1, other_down1 = shift(other, "z", 1), shift(other, "z", -1)
    up2, down2 = shift(up1, "z", 1), shift(down1, "z", -1)
    up3, down3 = shift(up2, "z", 1), shift(down2, "z", -1)
    w = own.shape[0] // 4
    fourth_up = shift(jnp.concatenate([up3[:w], up3[2 * w : 3 * w]], axis=0), "z", 1)
    fourth_down = shift(jnp.concatenate([down3[w : 2 * w], down3[3 * w :]], axis=0), "z", -1)
    fourth = jnp.concatenate([fourth_up[:w], fourth_down[:w], fourth_up[w:], fourth_down[w:]], axis=0)

    across = jnp.concatenate([shift(left[:quarter], "y", 1), shift(right[quarter:], "y", -1)], axis=0)
    near = [pool_embeds, left, swap_core(left), right, swap_core(right)]
    far = [across, swap_core(across)]
    early = [own, other, up1, down1, other_up1, other_down1, up2, down2]
    late = [swap_x(up2), swap_x(down2), up3, down3, swap_x(up3), swap_x(down3), fourth, swap_x(fourth)]
    first = lse_call(near, early, scale)
    second = lse_call(near, late, scale)
    place = jnp.stack([lax.axis_index("y"), core]).astype(jnp.int32)
    send = lse_call(far, early + late, scale, (first, second), place)

    got = lax.all_to_all(send, ROW_GROUP, 0, 0)
    pool_norms = jnp.sum(jnp.square(pool_embeds.astype(jnp.float32)), axis=1) * (KERNEL_GAIN / depth)
    dense = (count // 128, 128)
    blocks = lax.axis_size(BLK)
    log_ratio, stats = pl.pallas_call(
        merge_kernel,
        out_shape=(jax.ShapeDtypeStruct(dense, jnp.float32), jax.ShapeDtypeStruct((blocks, 128), jnp.float32)),
        in_specs=[VMEM, VMEM],
        out_specs=(VMEM, VMEM),
    )(got, pool_norms.reshape(dense))
    stats = lax.all_to_all(stats, BLK, 0, 0, tiled=True)
    standardized = pl.pallas_call(
        finish_kernel, out_shape=jax.ShapeDtypeStruct(dense, jnp.float32), in_specs=[VMEM, VMEM], out_specs=VMEM
    )(log_ratio, stats)
    return (log_ratio.reshape(count), standardized.reshape(count))


def solution(mesh):
    fine = Mesh(mesh.devices.reshape(2, 4, 8, 2, 2), ("xh", "y", "z", "xl", "core"))
    rows = P(BLK, None)
    samples = P(("xh", "y", "z", "xl", "core"), None)
    return jax.shard_map(
        body, mesh=fine, in_specs=(rows, samples, samples), out_specs=(P(BLK), P(BLK)), check_vma=False
    )
```

```python
import functools

import jax
import jax.numpy as jnp
from jax import lax
from jax.experimental import pallas as pl
from jax.experimental.pallas import tpu as pltpu
from jax.sharding import Mesh, PartitionSpec as P


KERNEL_GAIN = 30.0
TILE = 256
CHUNK = 256
SIZES = {"xh": 2, "y": 4, "z": 8, "xl": 2, "core": 2}
ROW_GROUP = ("y", "xl", "core")
BLK = ("xh", "y", "z")
VMEM = pl.BlockSpec(memory_space=pltpu.VMEM)


def lse_tiles(pools, samples, scale, out_ref, joined, half_norm, pool_all, bufs, tops):
    rows = joined.shape[0]
    member = rows // 2
    each = samples[0].shape[0] // 2
    for i, ref in enumerate(samples):
        joined[i * each : (i + 1) * each, :] = ref[:each, :]
        joined[member + i * each : member + (i + 1) * each, :] = ref[each:, :]
    count = 0
    for ref in pools:
        pool_all[count : count + ref.shape[0], :] = ref[...]
        count += ref.shape[0]

    def norms(i, _):
        at = pl.ds(pl.multiple_of(i * 128, 128), 128)
        wide = joined[at, :].astype(jnp.float32)
        half_norm[at, :] = jnp.broadcast_to(jnp.sum(wide * wide, axis=1, keepdims=True) * 0.5, (128, 128))
        return 0

    lax.fori_loop(0, rows // 128, norms, 0)
    tiles = count // TILE

    def step(tile, buf, top, done, done_buf, done_top):
        if tile is not None:
            weights = pool_all[pl.ds(pl.multiple_of(tile * TILE, TILE), TILE), :]
        if done is not None:
            high = [jnp.max(done_top[8 * m : 8 * m + 8, :], axis=0, keepdims=True) for m in range(2)]
        highs, totals = [None, None], [None, None]
        for c in range(rows // CHUNK):
            m = c * CHUNK // member
            at = slice(c * CHUNK, (c + 1) * CHUNK)
            if tile is not None:
                products = lax.dot_general(
                    joined[at, :], weights, (((1,), (1,)), ((), ())), preferred_element_type=jnp.float32
                )
                values = products - jnp.concatenate([half_norm[at, :]] * (TILE // 128), axis=1)
                buf[at, :] = values
                top_of = jnp.max(values.reshape(CHUNK // 8, 8, TILE), axis=0)
                highs[m] = top_of if highs[m] is None else jnp.maximum(highs[m], top_of)
            if done is not None:
                powers = jnp.exp((done_buf[at, :] - high[m]) * scale)
                total = jnp.sum(powers.reshape(CHUNK // 8, 8, TILE), axis=0)
                totals[m] = total if totals[m] is None else totals[m] + total
        if tile is not None:
            for m in range(2):
                top[8 * m : 8 * m + 8, :] = highs[m]
        if done is not None:
            for m in range(2):
                value = high[m] * scale + jnp.log(jnp.sum(totals[m], axis=0, keepdims=True))
                for k in range(TILE // 128):
                    out_ref[m, pl.ds(done * (TILE // 128) + k, 1), :] = value[:, k * 128 : (k + 1) * 128]

    step(0, bufs[0], tops[0], None, None, None)

    def pair(i, _):
        step(2 * i + 1, bufs[1], tops[1], 2 * i, bufs[0], tops[0])
        step(2 * i + 2, bufs[0], tops[0], 2 * i + 1, bufs[1], tops[1])
        return 0

    lax.fori_loop(0, tiles // 2 - 1, pair, 0)
    step(tiles - 1, bufs[1], tops[1], tiles - 2, bufs[0], tops[0])
    step(None, None, None, tiles - 1, bufs[1], tops[1])


def partial_kernel(n_pools, n_samples, scale, *refs):
    pools, samples, out_ref = refs[:n_pools], refs[n_pools : n_pools + n_samples], refs[n_pools + n_samples]
    joined, half_norm, pool_all, buf0, buf1, top0, top1 = refs[n_pools + n_samples + 1 :]
    lse_tiles(pools, samples, scale, out_ref, joined, half_norm, pool_all, (buf0, buf1), (top0, top1))


def add_exp(a, b):
    high = jnp.maximum(a, b)
    return high + jnp.log(jnp.exp(a - high) + jnp.exp(b - high))


def last_kernel(n_pools, n_samples, scale, place, *refs):
    pools, samples = refs[:n_pools], refs[n_pools : n_pools + n_samples]
    first, second, out_ref, across = refs[n_pools + n_samples : n_pools + n_samples + 4]
    joined, half_norm, pool_all, buf0, buf1, top0, top1 = refs[n_pools + n_samples + 4 :]
    lse_tiles(pools, samples, scale, across, joined, half_norm, pool_all, (buf0, buf1), (top0, top1))
    y, core = place[0], place[1]
    near = add_exp(first[...], second[...])
    n = near.shape[1] // 3
    far = across[...]

    def put(owner, value, swapped):
        half = n // 2
        for j in range(4):
            at = lax.rem(owner, 4) * 4 + j
            if swapped:
                out_ref[at, :, pl.ds(core * half, half), :] = value[:, :half, :]
                out_ref[at, :, pl.ds((1 - core) * half, half), :] = value[:, half:, :]
            else:
                out_ref[at, :, :, :] = value

    put(y, near[:, :n, :], False)
    put(y + 3, near[:, n : 2 * n, :], True)
    put(y + 1, near[:, 2 * n :, :], True)
    put(y + 2, far, True)


def lse_call(pools, samples, scale, earlier=None, place=None):
    count = sum(p.shape[0] for p in pools)
    rows = sum(s.shape[0] for s in samples)
    depth = pools[0].shape[1]
    scratch = [
        pltpu.VMEM((rows, depth), jnp.bfloat16),
        pltpu.VMEM((rows, 128), jnp.float32),
        pltpu.VMEM((count, depth), jnp.bfloat16),
        pltpu.VMEM((rows, TILE), jnp.float32),
        pltpu.VMEM((rows, TILE), jnp.float32),
        pltpu.VMEM((16, TILE), jnp.float32),
        pltpu.VMEM((16, TILE), jnp.float32),
    ]
    partial = jax.ShapeDtypeStruct((2, count // 128, 128), jnp.float32)
    common = dict(
        out_specs=VMEM,
        compiler_params=pltpu.CompilerParams(vmem_limit_bytes=30 * 1024 * 1024),
        cost_estimate=pl.CostEstimate(
            flops=2 * rows * count * depth, bytes_accessed=2 * (rows + count) * depth, transcendentals=rows * count
        ),
    )
    inputs = [VMEM] * (len(pools) + len(samples))
    if earlier is None:
        kernel = functools.partial(partial_kernel, len(pools), len(samples), scale)
        return pl.pallas_call(kernel, out_shape=partial, in_specs=inputs, scratch_shapes=scratch, **common)(*pools, *samples)
    kernel = functools.partial(last_kernel, len(pools), len(samples), scale)
    return pl.pallas_call(
        kernel,
        out_shape=jax.ShapeDtypeStruct((16,) + partial.shape, jnp.float32),
        in_specs=[pl.BlockSpec(memory_space=pltpu.SMEM)] + inputs + [VMEM] * 2,
        scratch_shapes=[pltpu.VMEM(partial.shape, jnp.float32)] + scratch,
        **common,
    )(place, *pools, *samples, *earlier)


def merge_kernel(got, norms, ratio_ref, stats_ref):
    value = got[...]
    high = jnp.max(value, axis=0)
    total = high + jnp.log(jnp.sum(jnp.exp(value - high[None]), axis=0))
    log_target = total[0] - norms[...]
    log_ref = total[1] - norms[...]
    ratio = log_target - log_ref
    ratio_ref[...] = ratio
    count = ratio.shape[0] * ratio.shape[1]
    mean = jnp.sum(ratio, axis=(0, 1), keepdims=True) / count
    square = jnp.sum(jnp.square(ratio - mean), axis=(0, 1), keepdims=True) / count
    lane = lax.broadcasted_iota(jnp.int32, stats_ref.shape, 1)
    stats_ref[...] = jnp.where(lane == 0, mean, jnp.where(lane == 1, square, 0.0))


def finish_kernel(ratio, stats, out_ref):
    blocks = stats.shape[0]
    value = stats[...]
    mean = jnp.sum(value[:, 0:1], axis=0, keepdims=True) / blocks
    variance = jnp.sum(value[:, 1:2] + jnp.square(value[:, 0:1] - mean), axis=0, keepdims=True) / blocks
    out_ref[...] = (ratio[...] - mean) / jnp.sqrt(variance + 1e-05)


def shift(value, axis, by):
    n = SIZES[axis]
    return lax.ppermute(value, axis, [(i, (i + by) % n) for i in range(n)])


def swap_core(value):
    return lax.ppermute(value, "core", [(0, 1), (1, 0)])


def swap_x(value):
    return lax.ppermute(value, ("xh", "xl"), [(0, 3), (3, 0), (1, 2), (2, 1)])


def stage_kernel(place, pool, target, reference, mine, own, sems):
    half, each = mine.shape[0], target.shape[0]
    copies = [
        pltpu.make_async_copy(pool.at[pl.ds(pl.multiple_of(place[1] * half, half), half), :], mine, sems.at[0]),
        pltpu.make_async_copy(target, own.at[pl.ds(0, each), :], sems.at[1]),
        pltpu.make_async_copy(reference, own.at[pl.ds(each, each), :], sems.at[2]),
    ]
    for copy in copies:
        copy.start()
    for copy in copies:
        copy.wait()


def body(pool_embeds, target_samples, reference_samples):
    count, depth = pool_embeds.shape
    half = count // 2
    quarter = half // 2
    core = lax.axis_index("core")
    scale = 2.0 * KERNEL_GAIN / depth

    place = jnp.stack([lax.axis_index("y"), core]).astype(jnp.int32)
    anywhere = pl.BlockSpec(memory_space=pl.ANY)
    mine, own = pl.pallas_call(
        stage_kernel,
        out_shape=(
            jax.ShapeDtypeStruct((half, depth), pool_embeds.dtype),
            jax.ShapeDtypeStruct((2 * target_samples.shape[0], depth), target_samples.dtype),
        ),
        in_specs=[pl.BlockSpec(memory_space=pltpu.SMEM)] + [anywhere] * 3,
        out_specs=(VMEM, VMEM),
        scratch_shapes=[pltpu.SemaphoreType.DMA((3,))],
    )(place, pool_embeds, target_samples, reference_samples)
    left, right = shift(mine, "y", 1), shift(mine, "y", -1)
    other = swap_x(own)
    up1, down1 = shift(own, "z", 1), shift(own, "z", -1)
    far_block = shift(own, "z", 4)
    other_up1, other_down1 = shift(other, "z", 1), shift(other, "z", -1)
    up2, down2 = shift(up1, "z", 1), shift(down1, "z", -1)
    up3, down3 = shift(up2, "z", 1), shift(down2, "z", -1)

    across_left = shift(left[:quarter], "y", 1)
    across_right = shift(right[quarter:], "y", -1)
    near = [pool_embeds, left, swap_core(left), right, swap_core(right)]
    far = [across_left, across_right, swap_core(across_left), swap_core(across_right)]
    early = [own, other, up1, down1, other_up1, other_down1, up2, down2]
    late = [swap_x(up2), swap_x(down2), up3, down3]
    late += [swap_x(up3), swap_x(down3), far_block, swap_x(far_block)]
    first = lse_call(near, early, scale)
    second = lse_call(near, late, scale)
    send = lse_call(far, early + late, scale, (first, second), place)

    got = lax.all_to_all(send, ROW_GROUP, 0, 0)
    pool_norms = jnp.sum(jnp.square(pool_embeds.astype(jnp.float32)), axis=1) * (KERNEL_GAIN / depth)
    dense = (count // 128, 128)
    blocks = lax.axis_size(BLK)
    log_ratio, stats = pl.pallas_call(
        merge_kernel,
        out_shape=(jax.ShapeDtypeStruct(dense, jnp.float32), jax.ShapeDtypeStruct((blocks, 128), jnp.float32)),
        in_specs=[VMEM, VMEM],
        out_specs=(VMEM, VMEM),
    )(got, pool_norms.reshape(dense))
    stats = lax.all_to_all(stats, BLK, 0, 0, tiled=True)
    standardized = pl.pallas_call(
        finish_kernel, out_shape=jax.ShapeDtypeStruct(dense, jnp.float32), in_specs=[VMEM, VMEM], out_specs=VMEM
    )(log_ratio, stats)
    return (log_ratio.reshape(count), standardized.reshape(count))


def solution(mesh):
    fine = Mesh(mesh.devices.reshape(2, 4, 8, 2, 2), ("xh", "y", "z", "xl", "core"))
    rows = P(BLK, None)
    samples = P(("xh", "y", "z", "xl", "core"), None)
    return jax.shard_map(
        body, mesh=fine, in_specs=(rows, samples, samples), out_specs=(P(BLK), P(BLK)), check_vma=False
    )
```

```python
import functools

import jax
import jax.numpy as jnp
from jax import lax
from jax.experimental import pallas as pl
from jax.experimental.pallas import tpu as pltpu
from jax.sharding import Mesh, PartitionSpec as P


KERNEL_GAIN = 30.0
TILE = 256
CHUNK = 256
SIZES = {"xh": 2, "y": 4, "z": 8, "xl": 2, "core": 2}
ROW_GROUP = ("y", "xl", "core")
BLK = ("xh", "y", "z")
VMEM = pl.BlockSpec(memory_space=pltpu.VMEM)


def lse_tiles(pools, samples, each, scale, out_ref, joined, half_norm, pool_all, bufs, tops):
    rows = joined.shape[0]
    member = rows // 2
    i = 0
    for ref in samples:
        for unit in range(0, ref.shape[0], 2 * each):
            joined[i * each : (i + 1) * each, :] = ref[unit : unit + each, :]
            joined[member + i * each : member + (i + 1) * each, :] = ref[unit + each : unit + 2 * each, :]
            i += 1
    count = 0
    for ref in pools:
        pool_all[count : count + ref.shape[0], :] = ref[...]
        count += ref.shape[0]

    def norms(i, _):
        at = pl.ds(pl.multiple_of(i * 128, 128), 128)
        wide = joined[at, :].astype(jnp.float32)
        half_norm[at, :] = jnp.broadcast_to(jnp.sum(wide * wide, axis=1, keepdims=True) * 0.5, (128, 128))
        return 0

    lax.fori_loop(0, rows // 128, norms, 0)
    tiles = count // TILE

    def step(tile, buf, top, done, done_buf, done_top):
        if tile is not None:
            weights = pool_all[pl.ds(pl.multiple_of(tile * TILE, TILE), TILE), :]
        if done is not None:
            high = [jnp.max(done_top[8 * m : 8 * m + 8, :], axis=0, keepdims=True) for m in range(2)]
        highs, totals = [None, None], [None, None]
        for c in range(rows // CHUNK):
            m = c * CHUNK // member
            at = slice(c * CHUNK, (c + 1) * CHUNK)
            if tile is not None:
                products = lax.dot_general(
                    joined[at, :], weights, (((1,), (1,)), ((), ())), preferred_element_type=jnp.float32
                )
                values = products - jnp.concatenate([half_norm[at, :]] * (TILE // 128), axis=1)
                buf[at, :] = values
                top_of = jnp.max(values.reshape(CHUNK // 8, 8, TILE), axis=0)
                highs[m] = top_of if highs[m] is None else jnp.maximum(highs[m], top_of)
            if done is not None:
                powers = jnp.exp((done_buf[at, :] - high[m]) * scale)
                total = jnp.sum(powers.reshape(CHUNK // 8, 8, TILE), axis=0)
                totals[m] = total if totals[m] is None else totals[m] + total
        if tile is not None:
            for m in range(2):
                top[8 * m : 8 * m + 8, :] = highs[m]
        if done is not None:
            for m in range(2):
                value = high[m] * scale + jnp.log(jnp.sum(totals[m], axis=0, keepdims=True))
                for k in range(TILE // 128):
                    out_ref[m, pl.ds(done * (TILE // 128) + k, 1), :] = value[:, k * 128 : (k + 1) * 128]

    step(0, bufs[0], tops[0], None, None, None)

    def pair(i, _):
        step(2 * i + 1, bufs[1], tops[1], 2 * i, bufs[0], tops[0])
        step(2 * i + 2, bufs[0], tops[0], 2 * i + 1, bufs[1], tops[1])
        return 0

    lax.fori_loop(0, tiles // 2 - 1, pair, 0)
    step(tiles - 1, bufs[1], tops[1], tiles - 2, bufs[0], tops[0])
    step(None, None, None, tiles - 1, bufs[1], tops[1])


def partial_kernel(n_pools, n_samples, each, scale, *refs):
    pools, samples, out_ref = refs[:n_pools], refs[n_pools : n_pools + n_samples], refs[n_pools + n_samples]
    joined, half_norm, pool_all, buf0, buf1, top0, top1 = refs[n_pools + n_samples + 1 :]
    lse_tiles(pools, samples, each, scale, out_ref, joined, half_norm, pool_all, (buf0, buf1), (top0, top1))


def add_exp(a, b):
    high = jnp.maximum(a, b)
    return high + jnp.log(jnp.exp(a - high) + jnp.exp(b - high))


def last_kernel(n_pools, n_samples, each, scale, place, *refs):
    pools, samples = refs[:n_pools], refs[n_pools : n_pools + n_samples]
    first, second, out_ref, across = refs[n_pools + n_samples : n_pools + n_samples + 4]
    joined, half_norm, pool_all, buf0, buf1, top0, top1 = refs[n_pools + n_samples + 4 :]
    lse_tiles(pools, samples, each, scale, across, joined, half_norm, pool_all, (buf0, buf1), (top0, top1))
    y, core = place[0], place[1]
    near = add_exp(first[...], second[...])
    n = near.shape[1] // 3
    far = across[...]

    def put(owner, value, swapped):
        half = n // 2
        for j in range(4):
            at = lax.rem(owner, 4) * 4 + j
            if swapped:
                out_ref[at, :, pl.ds(core * half, half), :] = value[:, :half, :]
                out_ref[at, :, pl.ds((1 - core) * half, half), :] = value[:, half:, :]
            else:
                out_ref[at, :, :, :] = value

    put(y, near[:, :n, :], False)
    put(y + 3 - 2 * core, near[:, n : 2 * n, :], False)
    put(y + 1 + 2 * core, near[:, 2 * n :, :], False)
    put(y + 2, far, True)


def lse_call(pools, samples, each, scale, earlier=None, place=None):
    count = sum(p.shape[0] for p in pools)
    rows = sum(s.shape[0] for s in samples)
    depth = pools[0].shape[1]
    scratch = [
        pltpu.VMEM((rows, depth), jnp.bfloat16),
        pltpu.VMEM((rows, 128), jnp.float32),
        pltpu.VMEM((count, depth), jnp.bfloat16),
        pltpu.VMEM((rows, TILE), jnp.float32),
        pltpu.VMEM((rows, TILE), jnp.float32),
        pltpu.VMEM((16, TILE), jnp.float32),
        pltpu.VMEM((16, TILE), jnp.float32),
    ]
    partial = jax.ShapeDtypeStruct((2, count // 128, 128), jnp.float32)
    common = dict(
        out_specs=VMEM,
        compiler_params=pltpu.CompilerParams(vmem_limit_bytes=14 * 1024 * 1024),
        cost_estimate=pl.CostEstimate(
            flops=2 * rows * count * depth, bytes_accessed=2 * (rows + count) * depth, transcendentals=rows * count
        ),
    )
    inputs = [VMEM] * (len(pools) + len(samples))
    if earlier is None:
        kernel = functools.partial(partial_kernel, len(pools), len(samples), each, scale)
        return pl.pallas_call(kernel, out_shape=partial, in_specs=inputs, scratch_shapes=scratch, **common)(*pools, *samples)
    kernel = functools.partial(last_kernel, len(pools), len(samples), each, scale)
    return pl.pallas_call(
        kernel,
        out_shape=jax.ShapeDtypeStruct((16,) + partial.shape, jnp.float32),
        in_specs=[pl.BlockSpec(memory_space=pltpu.SMEM)] + inputs + [VMEM] * 2,
        scratch_shapes=[pltpu.VMEM(partial.shape, jnp.float32)] + scratch,
        **common,
    )(place, *pools, *samples, *earlier)


def merge_kernel(got, norms, ratio_ref, stats_ref):
    value = got[...]
    high = jnp.max(value, axis=0)
    total = high + jnp.log(jnp.sum(jnp.exp(value - high[None]), axis=0))
    log_target = total[0] - norms[...]
    log_ref = total[1] - norms[...]
    ratio = log_target - log_ref
    ratio_ref[...] = ratio
    count = ratio.shape[0] * ratio.shape[1]
    mean = jnp.sum(ratio, axis=(0, 1), keepdims=True) / count
    square = jnp.sum(jnp.square(ratio - mean), axis=(0, 1), keepdims=True) / count
    lane = lax.broadcasted_iota(jnp.int32, stats_ref.shape, 1)
    stats_ref[...] = jnp.where(lane == 0, mean, jnp.where(lane == 1, square, 0.0))


def finish_kernel(ratio, stats, out_ref):
    blocks = stats.shape[0]
    value = stats[...]
    mean = jnp.sum(value[:, 0:1], axis=0, keepdims=True) / blocks
    variance = jnp.sum(value[:, 1:2] + jnp.square(value[:, 0:1] - mean), axis=0, keepdims=True) / blocks
    out_ref[...] = (ratio[...] - mean) / jnp.sqrt(variance + 1e-05)


def swap_core(value):
    return lax.ppermute(value, "core", [(0, 1), (1, 0)])


def swap_x(value):
    return lax.ppermute(value, ("xh", "xl"), [(0, 3), (3, 0), (1, 2), (2, 1)])


def both_ways(value, axis):
    n = SIZES[axis]
    pairs = [(2 * i, 2 * ((i + 1) % n)) for i in range(n)] + [(2 * i + 1, 2 * ((i - 1) % n) + 1) for i in range(n)]
    return lax.ppermute(value, (axis, "core"), pairs)


def body(pool_embeds, target_samples, reference_samples):
    count, depth = pool_embeds.shape
    half = count // 2
    core = lax.axis_index("core")
    each = target_samples.shape[0]
    scale = 2.0 * KERNEL_GAIN / depth
    place = jnp.stack([lax.axis_index("y"), core]).astype(jnp.int32)

    own = jnp.concatenate([target_samples, reference_samples], axis=0)
    beside = both_ways(pool_embeds, "y")
    other = swap_x(own)
    block = jnp.concatenate([own, swap_core(own)], axis=0)
    z1 = both_ways(block, "z")
    other_block = jnp.concatenate([other, swap_core(other)], axis=0)
    zx1 = both_ways(other_block, "z")
    z2 = both_ways(z1, "z")
    zx2 = both_ways(zx1, "z")
    z3 = both_ways(z2, "z")
    zx3 = both_ways(zx2, "z")
    z4 = both_ways(z3[: 2 * each], "z")
    across = both_ways(lax.dynamic_slice_in_dim(beside, core * half, half, 0), "y")
    near = [pool_embeds, beside, swap_core(beside)]
    far = [across, swap_core(across)]
    early = [own, other, z1, zx1, z2]
    late = [zx2, z3, zx3, z4, swap_x(z4)]
    first = lse_call(near, early, each, scale)
    second = lse_call(near, late, each, scale)
    send = lse_call(far, early + late, each, scale, (first, second), place)

    got = lax.all_to_all(send, ROW_GROUP, 0, 0)
    pool_norms = jnp.sum(jnp.square(pool_embeds.astype(jnp.float32)), axis=1) * (KERNEL_GAIN / depth)
    dense = (count // 128, 128)
    blocks = lax.axis_size(BLK)
    log_ratio, stats = pl.pallas_call(
        merge_kernel,
        out_shape=(jax.ShapeDtypeStruct(dense, jnp.float32), jax.ShapeDtypeStruct((blocks, 128), jnp.float32)),
        in_specs=[VMEM, VMEM],
        out_specs=(VMEM, VMEM),
    )(got, pool_norms.reshape(dense))
    stats = lax.all_to_all(stats, BLK, 0, 0, tiled=True)
    standardized = pl.pallas_call(
        finish_kernel, out_shape=jax.ShapeDtypeStruct(dense, jnp.float32), in_specs=[VMEM, VMEM], out_specs=VMEM
    )(log_ratio, stats)
    return (log_ratio.reshape(count), standardized.reshape(count))


def solution(mesh):
    fine = Mesh(mesh.devices.reshape(2, 4, 8, 2, 2), ("xh", "y", "z", "xl", "core"))
    rows = P(BLK, None)
    samples = P(("xh", "y", "z", "xl", "core"), None)
    return jax.shard_map(
        body, mesh=fine, in_specs=(rows, samples, samples), out_specs=(P(BLK), P(BLK)), check_vma=False
    )
```

```python
import functools

import jax
import jax.numpy as jnp
from jax import lax
from jax.experimental import pallas as pl
from jax.experimental.pallas import tpu as pltpu
from jax.sharding import Mesh, PartitionSpec as P


KERNEL_GAIN = 30.0
TILE = 256
CHUNK = 384
SIZES = {"xh": 2, "y": 4, "z": 8, "xl": 2, "core": 2}
ROW_GROUP = ("y", "xl", "core")
BLK = ("xh", "y", "z")
VMEM = pl.BlockSpec(memory_space=pltpu.VMEM)


def lse_tiles(pools, samples, each, scale, out_ref, joined, half_norm, pool_all, bufs, tops):
    rows = joined.shape[0]
    member = rows // 2
    i = 0
    for ref in samples:
        for unit in range(0, ref.shape[0], 2 * each):
            joined[i * each : (i + 1) * each, :] = ref[unit : unit + each, :]
            joined[member + i * each : member + (i + 1) * each, :] = ref[unit + each : unit + 2 * each, :]
            i += 1
    count = 0
    for ref in pools:
        pool_all[count : count + ref.shape[0], :] = ref[...]
        count += ref.shape[0]

    def norms(i, _):
        at = pl.ds(pl.multiple_of(i * 128, 128), 128)
        wide = joined[at, :].astype(jnp.float32)
        half_norm[at, :] = jnp.broadcast_to(jnp.sum(wide * wide, axis=1, keepdims=True) * 0.5, (128, 128))
        return 0

    lax.fori_loop(0, rows // 128, norms, 0)
    tiles = count // TILE
    chunk = member // -(-member // CHUNK)

    def step(tile, buf, top, done, done_buf, done_top):
        if tile is not None:
            weights = pool_all[pl.ds(pl.multiple_of(tile * TILE, TILE), TILE), :]
        if done is not None:
            high = [jnp.max(done_top[8 * m : 8 * m + 8, :], axis=0, keepdims=True) for m in range(2)]
        highs, totals = [None, None], [None, None]
        for c in range(rows // chunk):
            m = c * chunk // member
            at = slice(c * chunk, (c + 1) * chunk)
            if tile is not None:
                products = lax.dot_general(
                    joined[at, :], weights, (((1,), (1,)), ((), ())), preferred_element_type=jnp.float32
                )
                values = products - jnp.concatenate([half_norm[at, :]] * (TILE // 128), axis=1)
                buf[at, :] = values
                top_of = jnp.max(values.reshape(chunk // 8, 8, TILE), axis=0)
                highs[m] = top_of if highs[m] is None else jnp.maximum(highs[m], top_of)
            if done is not None:
                powers = jnp.exp((done_buf[at, :] - high[m]) * scale)
                total = jnp.sum(powers.reshape(chunk // 8, 8, TILE), axis=0)
                totals[m] = total if totals[m] is None else totals[m] + total
        if tile is not None:
            for m in range(2):
                top[8 * m : 8 * m + 8, :] = highs[m]
        if done is not None:
            for m in range(2):
                value = high[m] * scale + jnp.log(jnp.sum(totals[m], axis=0, keepdims=True))
                for k in range(TILE // 128):
                    out_ref[m, pl.ds(done * (TILE // 128) + k, 1), :] = value[:, k * 128 : (k + 1) * 128]

    step(0, bufs[0], tops[0], None, None, None)

    def pair(i, _):
        step(2 * i + 1, bufs[1], tops[1], 2 * i, bufs[0], tops[0])
        step(2 * i + 2, bufs[0], tops[0], 2 * i + 1, bufs[1], tops[1])
        return 0

    lax.fori_loop(0, tiles // 2 - 1, pair, 0)
    step(tiles - 1, bufs[1], tops[1], tiles - 2, bufs[0], tops[0])
    step(None, None, None, tiles - 1, bufs[1], tops[1])


def partial_kernel(n_pools, n_samples, each, scale, *refs):
    pools, samples, out_ref = refs[:n_pools], refs[n_pools : n_pools + n_samples], refs[n_pools + n_samples]
    joined, half_norm, pool_all, buf0, buf1, top0, top1 = refs[n_pools + n_samples + 1 :]
    lse_tiles(pools, samples, each, scale, out_ref, joined, half_norm, pool_all, (buf0, buf1), (top0, top1))


def add_exp(a, b):
    high = jnp.maximum(a, b)
    return high + jnp.log(jnp.exp(a - high) + jnp.exp(b - high))


def last_kernel(n_pools, n_samples, each, scale, place, *refs):
    pools, samples = refs[:n_pools], refs[n_pools : n_pools + n_samples]
    first, second, third, out_ref, last = refs[n_pools + n_samples : n_pools + n_samples + 5]
    joined, half_norm, pool_all, buf0, buf1, top0, top1 = refs[n_pools + n_samples + 5 :]
    lse_tiles(pools, samples, each, scale, last, joined, half_norm, pool_all, (buf0, buf1), (top0, top1))
    y, core = place[0], place[1]
    n = first.shape[1] // 3
    near = add_exp(add_exp(first[...], second[...]), last[:, : 3 * n, :])
    far = add_exp(third[...], last[:, 3 * n :, :])

    def put(owner, value, swapped):
        half = n // 2
        for j in range(4):
            at = lax.rem(owner, 4) * 4 + j
            if swapped:
                out_ref[at, :, pl.ds(core * half, half), :] = value[:, :half, :]
                out_ref[at, :, pl.ds((1 - core) * half, half), :] = value[:, half:, :]
            else:
                out_ref[at, :, :, :] = value

    put(y, near[:, :n, :], False)
    put(y + 3 - 2 * core, near[:, n : 2 * n, :], False)
    put(y + 1 + 2 * core, near[:, 2 * n :, :], False)
    put(y + 2, far, True)


def lse_call(pools, samples, each, scale, earlier=None, place=None):
    count = sum(p.shape[0] for p in pools)
    rows = sum(s.shape[0] for s in samples)
    depth = pools[0].shape[1]
    scratch = [
        pltpu.VMEM((rows, depth), jnp.bfloat16),
        pltpu.VMEM((rows, 128), jnp.float32),
        pltpu.VMEM((count, depth), jnp.bfloat16),
        pltpu.VMEM((rows, TILE), jnp.float32),
        pltpu.VMEM((rows, TILE), jnp.float32),
        pltpu.VMEM((16, TILE), jnp.float32),
        pltpu.VMEM((16, TILE), jnp.float32),
    ]
    partial = jax.ShapeDtypeStruct((2, count // 128, 128), jnp.float32)
    common = dict(
        out_specs=VMEM,
        compiler_params=pltpu.CompilerParams(vmem_limit_bytes=14 * 1024 * 1024),
        cost_estimate=pl.CostEstimate(
            flops=2 * rows * count * depth, bytes_accessed=2 * (rows + count) * depth, transcendentals=rows * count
        ),
    )
    inputs = [VMEM] * (len(pools) + len(samples))
    if earlier is None:
        kernel = functools.partial(partial_kernel, len(pools), len(samples), each, scale)
        return pl.pallas_call(kernel, out_shape=partial, in_specs=inputs, scratch_shapes=scratch, **common)(*pools, *samples)
    kernel = functools.partial(last_kernel, len(pools), len(samples), each, scale)
    return pl.pallas_call(
        kernel,
        out_shape=jax.ShapeDtypeStruct((16, 2, pools[0].shape[0] // 128, 128), jnp.float32),
        in_specs=[pl.BlockSpec(memory_space=pltpu.SMEM)] + inputs + [VMEM] * len(earlier),
        scratch_shapes=[pltpu.VMEM(partial.shape, jnp.float32)] + scratch,
        **common,
    )(place, *pools, *samples, *earlier)


def merge_kernel(got, norms, ratio_ref, stats_ref):
    value = got[...]
    high = jnp.max(value, axis=0)
    total = high + jnp.log(jnp.sum(jnp.exp(value - high[None]), axis=0))
    log_target = total[0] - norms[...]
    log_ref = total[1] - norms[...]
    ratio = log_target - log_ref
    ratio_ref[...] = ratio
    count = ratio.shape[0] * ratio.shape[1]
    mean = jnp.sum(ratio, axis=(0, 1), keepdims=True) / count
    square = jnp.sum(jnp.square(ratio - mean), axis=(0, 1), keepdims=True) / count
    lane = lax.broadcasted_iota(jnp.int32, stats_ref.shape, 1)
    stats_ref[...] = jnp.where(lane == 0, mean, jnp.where(lane == 1, square, 0.0))


def finish_kernel(ratio, stats, out_ref):
    blocks = stats.shape[0]
    value = stats[...]
    mean = jnp.sum(value[:, 0:1], axis=0, keepdims=True) / blocks
    variance = jnp.sum(value[:, 1:2] + jnp.square(value[:, 0:1] - mean), axis=0, keepdims=True) / blocks
    out_ref[...] = (ratio[...] - mean) / jnp.sqrt(variance + 1e-05)


def swap_core(value):
    return lax.ppermute(value, "core", [(0, 1), (1, 0)])


def swap_x(value):
    return lax.ppermute(value, ("xh", "xl"), [(0, 3), (3, 0), (1, 2), (2, 1)])


def both_ways(value, axis):
    n = SIZES[axis]
    pairs = [(2 * i, 2 * ((i + 1) % n)) for i in range(n)] + [(2 * i + 1, 2 * ((i - 1) % n) + 1) for i in range(n)]
    return lax.ppermute(value, (axis, "core"), pairs)


def body(pool_embeds, target_samples, reference_samples):
    count, depth = pool_embeds.shape
    half = count // 2
    core = lax.axis_index("core")
    each = target_samples.shape[0]
    scale = 2.0 * KERNEL_GAIN / depth
    place = jnp.stack([lax.axis_index("y"), core]).astype(jnp.int32)

    own = jnp.where(
        lax.broadcasted_iota(jnp.int32, (2 * each, depth), 0) < each,
        jnp.pad(target_samples, ((0, each), (0, 0))),
        jnp.pad(reference_samples, ((each, 0), (0, 0))),
    )
    beside = both_ways(pool_embeds, "y")
    other = swap_x(own)
    block = jnp.concatenate([own, swap_core(own)], axis=0)
    z1 = both_ways(block, "z")
    other_block = jnp.concatenate([other, swap_core(other)], axis=0)
    zx1 = both_ways(other_block, "z")
    z2 = both_ways(z1, "z")
    zx2 = both_ways(zx1, "z")
    z3 = both_ways(z2, "z")
    zx3 = both_ways(zx2, "z")
    z4 = both_ways(z3[: 2 * each], "z")
    across = both_ways(lax.dynamic_slice_in_dim(beside, core * half, half, 0), "y")
    near = [pool_embeds, beside, swap_core(beside)]
    far = [across, swap_core(across)]
    earliest, early = [own, other, z1, zx1], [z2, zx2]
    late = [z3, zx3, z4, swap_x(z4)]
    first = lse_call(near, earliest, each, scale)
    second = lse_call(near, early, each, scale)
    third = lse_call(far, earliest + early, each, scale)
    send = lse_call(near + far, late, each, scale, (first, second, third), place)

    got = lax.all_to_all(send, ROW_GROUP, 0, 0)
    pool_norms = jnp.sum(jnp.square(pool_embeds.astype(jnp.float32)), axis=1) * (KERNEL_GAIN / depth)
    dense = (count // 128, 128)
    blocks = lax.axis_size(BLK)
    log_ratio, stats = pl.pallas_call(
        merge_kernel,
        out_shape=(jax.ShapeDtypeStruct(dense, jnp.float32), jax.ShapeDtypeStruct((blocks, 128), jnp.float32)),
        in_specs=[VMEM, VMEM],
        out_specs=(VMEM, VMEM),
    )(got, pool_norms.reshape(dense))
    stats = lax.all_to_all(stats, BLK, 0, 0, tiled=True)
    standardized = pl.pallas_call(
        finish_kernel, out_shape=jax.ShapeDtypeStruct(dense, jnp.float32), in_specs=[VMEM, VMEM], out_specs=VMEM
    )(log_ratio, stats)
    return (log_ratio.reshape(count), standardized.reshape(count))


def solution(mesh):
    fine = Mesh(mesh.devices.reshape(2, 4, 8, 2, 2), ("xh", "y", "z", "xl", "core"))
    rows = P(BLK, None)
    samples = P(("xh", "y", "z", "xl", "core"), None)
    return jax.shard_map(
        body, mesh=fine, in_specs=(rows, samples, samples), out_specs=(P(BLK), P(BLK)), check_vma=False
    )
```

```python
import functools

import jax
import jax.numpy as jnp
from jax import lax
from jax.experimental import pallas as pl
from jax.experimental.pallas import tpu as pltpu
from jax.sharding import Mesh, PartitionSpec as P


KERNEL_GAIN = 30.0
TILE = 256
CHUNK = 384
SIZES = {"xh": 2, "y": 4, "z": 8, "xl": 2, "core": 2}
ROW_GROUP = ("y", "xl", "core")
BLK = ("xh", "y", "z")
VMEM = pl.BlockSpec(memory_space=pltpu.VMEM)


def lse_tiles(pools, samples, each, scale, out_ref, joined, half_norm, pool_all, bufs, tops, sems):
    rows = joined.shape[0]
    member = rows // 2
    sample_copies, pool_copies = [], []
    for ref in samples:
        for unit in range(0, ref.shape[0], 2 * each):
            n = len(sample_copies)
            at = n // 2 * each
            for m in range(2):
                sample_copies.append(
                    pltpu.make_async_copy(
                        ref.at[pl.ds(unit + m * each, each), :], joined.at[pl.ds(at + m * member, each), :], sems.at[n + m]
                    )
                )
    count = 0
    for ref in pools:
        sem = sems.at[len(sample_copies) + len(pool_copies)]
        pool_copies.append(pltpu.make_async_copy(ref, pool_all.at[pl.ds(count, ref.shape[0]), :], sem))
        count += ref.shape[0]
    for copy in sample_copies + pool_copies:
        copy.start()
    for copy in sample_copies:
        copy.wait()

    def norms(i, _):
        at = pl.ds(pl.multiple_of(i * 128, 128), 128)
        wide = joined[at, :].astype(jnp.float32)
        half_norm[at, :] = jnp.broadcast_to(jnp.sum(wide * wide, axis=1, keepdims=True) * 0.5, (128, 128))
        return 0

    lax.fori_loop(0, rows // 128, norms, 0, unroll=True)
    pool_copies[0].wait()
    tiles = count // TILE
    chunk = member // -(-member // CHUNK)

    def step(tile, buf, top, done, done_buf, done_top):
        if tile is not None:
            weights = pool_all[pl.ds(pl.multiple_of(tile * TILE, TILE), TILE), :]
        if done is not None:
            high = [jnp.max(done_top[8 * m : 8 * m + 8, :], axis=0, keepdims=True) for m in range(2)]
        highs, totals = [None, None], [None, None]
        for c in range(rows // chunk):
            m = c * chunk // member
            at = slice(c * chunk, (c + 1) * chunk)
            if tile is not None:
                products = lax.dot_general(
                    joined[at, :], weights, (((1,), (1,)), ((), ())), preferred_element_type=jnp.float32
                )
                values = products - jnp.concatenate([half_norm[at, :]] * (TILE // 128), axis=1)
                buf[at, :] = values
                top_of = jnp.max(values.reshape(chunk // 8, 8, TILE), axis=0)
                highs[m] = top_of if highs[m] is None else jnp.maximum(highs[m], top_of)
            if done is not None:
                powers = jnp.exp((done_buf[at, :] - high[m]) * scale)
                total = jnp.sum(powers.reshape(chunk // 8, 8, TILE), axis=0)
                totals[m] = total if totals[m] is None else totals[m] + total
        if tile is not None:
            for m in range(2):
                top[8 * m : 8 * m + 8, :] = highs[m]
        if done is not None:
            for m in range(2):
                value = high[m] * scale + jnp.log(jnp.sum(totals[m], axis=0, keepdims=True))
                for k in range(TILE // 128):
                    out_ref[m, pl.ds(done * (TILE // 128) + k, 1), :] = value[:, k * 128 : (k + 1) * 128]

    step(0, bufs[0], tops[0], None, None, None)
    for copy in pool_copies[1:]:
        copy.wait()

    def pair(i, _):
        step(2 * i + 1, bufs[1], tops[1], 2 * i, bufs[0], tops[0])
        step(2 * i + 2, bufs[0], tops[0], 2 * i + 1, bufs[1], tops[1])
        return 0

    lax.fori_loop(0, tiles // 2 - 1, pair, 0)
    step(tiles - 1, bufs[1], tops[1], tiles - 2, bufs[0], tops[0])
    step(None, None, None, tiles - 1, bufs[1], tops[1])


def partial_kernel(n_pools, n_samples, each, scale, *refs):
    pools, samples, out_ref = refs[:n_pools], refs[n_pools : n_pools + n_samples], refs[n_pools + n_samples]
    joined, half_norm, pool_all, buf0, buf1, top0, top1, sems = refs[n_pools + n_samples + 1 :]
    lse_tiles(pools, samples, each, scale, out_ref, joined, half_norm, pool_all, (buf0, buf1), (top0, top1), sems)


def add_exp(a, b):
    high = jnp.maximum(a, b)
    return high + jnp.log(jnp.exp(a - high) + jnp.exp(b - high))


def last_kernel(n_pools, n_samples, each, scale, place, *refs):
    pools, samples = refs[:n_pools], refs[n_pools : n_pools + n_samples]
    alone, first, second, third, out_ref, last = refs[n_pools + n_samples : n_pools + n_samples + 6]
    joined, half_norm, pool_all, buf0, buf1, top0, top1, sems = refs[n_pools + n_samples + 6 :]
    lse_tiles(pools, samples, each, scale, last, joined, half_norm, pool_all, (buf0, buf1), (top0, top1), sems)
    y, core = place[0], place[1]
    n = alone.shape[1]
    rest = add_exp(second[...], last[:, : 3 * n, :])
    own = add_exp(alone[...], rest[:, :n, :])
    near = add_exp(first[...], rest[:, n:, :])
    far = add_exp(third[...], last[:, 3 * n :, :])

    def put(owner, value, swapped):
        half = n // 2
        for j in range(4):
            at = lax.rem(owner, 4) * 4 + j
            if swapped:
                out_ref[at, :, pl.ds(core * half, half), :] = value[:, :half, :]
                out_ref[at, :, pl.ds((1 - core) * half, half), :] = value[:, half:, :]
            else:
                out_ref[at, :, :, :] = value

    put(y, own, False)
    put(y + 3 - 2 * core, near[:, :n, :], False)
    put(y + 1 + 2 * core, near[:, n:, :], False)
    put(y + 2, far, True)


def lse_call(pools, samples, each, scale, earlier=None, place=None):
    count = sum(p.shape[0] for p in pools)
    rows = sum(s.shape[0] for s in samples)
    depth = pools[0].shape[1]
    scratch = [
        pltpu.VMEM((rows, depth), jnp.bfloat16),
        pltpu.VMEM((rows, 128), jnp.float32),
        pltpu.VMEM((count, depth), jnp.bfloat16),
        pltpu.VMEM((rows, TILE), jnp.float32),
        pltpu.VMEM((rows, TILE), jnp.float32),
        pltpu.VMEM((16, TILE), jnp.float32),
        pltpu.VMEM((16, TILE), jnp.float32),
        pltpu.SemaphoreType.DMA((rows // each + len(pools),)),
    ]
    partial = jax.ShapeDtypeStruct((2, count // 128, 128), jnp.float32)
    common = dict(
        out_specs=VMEM,
        compiler_params=pltpu.CompilerParams(vmem_limit_bytes=14 * 1024 * 1024),
        cost_estimate=pl.CostEstimate(
            flops=2 * rows * count * depth, bytes_accessed=2 * (rows + count) * depth, transcendentals=rows * count
        ),
    )
    inputs = [pl.BlockSpec(memory_space=pl.ANY)] * (len(pools) + len(samples))
    if earlier is None:
        kernel = functools.partial(partial_kernel, len(pools), len(samples), each, scale)
        return pl.pallas_call(kernel, out_shape=partial, in_specs=inputs, scratch_shapes=scratch, **common)(*pools, *samples)
    kernel = functools.partial(last_kernel, len(pools), len(samples), each, scale)
    return pl.pallas_call(
        kernel,
        out_shape=jax.ShapeDtypeStruct((16, 2, pools[0].shape[0] // 128, 128), jnp.float32),
        in_specs=[pl.BlockSpec(memory_space=pltpu.SMEM)] + inputs + [VMEM] * len(earlier),
        scratch_shapes=[pltpu.VMEM(partial.shape, jnp.float32)] + scratch,
        **common,
    )(place, *pools, *samples, *earlier)


def merge_kernel(got, norms, ratio_ref, stats_ref):
    value = got[...]
    high = jnp.max(value, axis=0)
    total = high + jnp.log(jnp.sum(jnp.exp(value - high[None]), axis=0))
    log_target = total[0] - norms[...]
    log_ref = total[1] - norms[...]
    ratio = log_target - log_ref
    ratio_ref[...] = ratio
    count = ratio.shape[0] * ratio.shape[1]
    mean = jnp.sum(ratio, axis=(0, 1), keepdims=True) / count
    square = jnp.sum(jnp.square(ratio - mean), axis=(0, 1), keepdims=True) / count
    lane = lax.broadcasted_iota(jnp.int32, stats_ref.shape, 1)
    stats_ref[...] = jnp.where(lane == 0, mean, jnp.where(lane == 1, square, 0.0))


def finish_kernel(ratio, stats, out_ref):
    blocks = stats.shape[0]
    value = stats[...]
    mean = jnp.sum(value[:, 0:1], axis=0, keepdims=True) / blocks
    variance = jnp.sum(value[:, 1:2] + jnp.square(value[:, 0:1] - mean), axis=0, keepdims=True) / blocks
    out_ref[...] = (ratio[...] - mean) / jnp.sqrt(variance + 1e-05)


def swap_core(value):
    return lax.ppermute(value, "core", [(0, 1), (1, 0)])


def swap_x(value):
    return lax.ppermute(value, ("xh", "xl"), [(0, 3), (3, 0), (1, 2), (2, 1)])


def both_ways(value, axis):
    n = SIZES[axis]
    pairs = [(2 * i, 2 * ((i + 1) % n)) for i in range(n)] + [(2 * i + 1, 2 * ((i - 1) % n) + 1) for i in range(n)]
    return lax.ppermute(value, (axis, "core"), pairs)


def body(pool_embeds, target_samples, reference_samples):
    count, depth = pool_embeds.shape
    half = count // 2
    core = lax.axis_index("core")
    each = target_samples.shape[0]
    scale = 2.0 * KERNEL_GAIN / depth
    place = jnp.stack([lax.axis_index("y"), core]).astype(jnp.int32)

    own = jnp.where(
        lax.broadcasted_iota(jnp.int32, (2 * each, depth), 0) < each,
        jnp.pad(target_samples, ((0, each), (0, 0))),
        jnp.pad(reference_samples, ((each, 0), (0, 0))),
    )
    beside = both_ways(pool_embeds, "y")
    other = swap_x(own)
    block = jnp.concatenate([own, swap_core(own)], axis=0)
    z1 = both_ways(block, "z")
    other_block = jnp.concatenate([other, swap_core(other)], axis=0)
    zx1 = both_ways(other_block, "z")
    z2 = both_ways(z1, "z")
    zx2 = both_ways(zx1, "z")
    z3 = both_ways(z2, "z")
    zx3 = both_ways(zx2, "z")
    z4 = both_ways(z3[: 2 * each], "z")
    across = both_ways(lax.dynamic_slice_in_dim(beside, core * half, half, 0), "y")
    near = [beside, swap_core(beside)]
    far = [across, swap_core(across)]
    earliest, early = [own, other, z1], [zx1, z2, zx2]
    late = [z3, zx3, z4, swap_x(z4)]
    alone = lse_call([pool_embeds], earliest, each, scale)
    first = lse_call(near, earliest, each, scale)
    second = lse_call([pool_embeds] + near, early, each, scale)
    third = lse_call(far, earliest + early, each, scale)
    send = lse_call([pool_embeds] + near + far, late, each, scale, (alone, first, second, third), place)

    got = lax.all_to_all(send, ROW_GROUP, 0, 0)
    pool_norms = jnp.sum(jnp.square(pool_embeds.astype(jnp.float32)), axis=1) * (KERNEL_GAIN / depth)
    dense = (count // 128, 128)
    blocks = lax.axis_size(BLK)
    log_ratio, stats = pl.pallas_call(
        merge_kernel,
        out_shape=(jax.ShapeDtypeStruct(dense, jnp.float32), jax.ShapeDtypeStruct((blocks, 128), jnp.float32)),
        in_specs=[VMEM, VMEM],
        out_specs=(VMEM, VMEM),
    )(got, pool_norms.reshape(dense))
    stats = lax.all_to_all(stats, BLK, 0, 0, tiled=True)
    standardized = pl.pallas_call(
        finish_kernel, out_shape=jax.ShapeDtypeStruct(dense, jnp.float32), in_specs=[VMEM, VMEM], out_specs=VMEM
    )(log_ratio, stats)
    return (log_ratio.reshape(count), standardized.reshape(count))


def solution(mesh):
    fine = Mesh(mesh.devices.reshape(2, 4, 8, 2, 2), ("xh", "y", "z", "xl", "core"))
    rows = P(BLK, None)
    samples = P(("xh", "y", "z", "xl", "core"), None)
    return jax.shard_map(
        body, mesh=fine, in_specs=(rows, samples, samples), out_specs=(P(BLK), P(BLK)), check_vma=False
    )
```

```python
import functools

import jax
import jax.numpy as jnp
from jax import lax
from jax.experimental import pallas as pl
from jax.experimental.pallas import tpu as pltpu
from jax.sharding import Mesh, PartitionSpec as P


KERNEL_GAIN = 30.0
TILE = 256
CHUNK = 384
STRAIGHT = 5
TOGETHER = 2
SIZES = {"xh": 2, "y": 4, "z": 8, "xl": 2, "core": 2}
ROW_GROUP = ("y", "xl", "core")
BLK = ("xh", "y", "z")
VMEM = pl.BlockSpec(memory_space=pltpu.VMEM)


def lse_tiles(pools, samples, each, scale, out_ref, joined, half_norm, pool_all, bufs, tops, sems):
    rows = joined.shape[0]
    member = rows // 2
    sample_copies, pool_copies = [], []
    for ref in samples:
        for unit in range(0, ref.shape[0], 2 * each):
            n = len(sample_copies)
            at = n // 2 * each
            for m in range(2):
                sample_copies.append(
                    pltpu.make_async_copy(
                        ref.at[pl.ds(unit + m * each, each), :], joined.at[pl.ds(at + m * member, each), :], sems.at[n + m]
                    )
                )
    count = 0
    for ref in pools:
        sem = sems.at[len(sample_copies) + len(pool_copies)]
        pool_copies.append(pltpu.make_async_copy(ref, pool_all.at[pl.ds(count, ref.shape[0]), :], sem))
        count += ref.shape[0]
    for copy in sample_copies + pool_copies:
        copy.start()
    for copy in sample_copies:
        copy.wait()

    def norms(i, _):
        at = pl.ds(pl.multiple_of(i * 128, 128), 128)
        wide = joined[at, :].astype(jnp.float32)
        half_norm[at, :] = jnp.broadcast_to(jnp.sum(wide * wide, axis=1, keepdims=True) * 0.5, (128, 128))
        return 0

    lax.fori_loop(0, rows // 128, norms, 0, unroll=True)
    pool_copies[0].wait()
    tiles = count // TILE
    chunk = member // -(-member // CHUNK)

    def step(tile, buf, top, done, done_buf, done_top):
        if tile is not None:
            weights = pool_all[pl.ds(pl.multiple_of(tile * TILE, TILE), TILE), :]
        if done is not None:
            high = [jnp.max(done_top[8 * m : 8 * m + 8, :], axis=0, keepdims=True) for m in range(2)]
        highs, totals = [None, None], [None, None]
        for c in range(rows // chunk):
            m = c * chunk // member
            at = slice(c * chunk, (c + 1) * chunk)
            if tile is not None:
                products = lax.dot_general(
                    joined[at, :], weights, (((1,), (1,)), ((), ())), preferred_element_type=jnp.float32
                )
                values = products - jnp.concatenate([half_norm[at, :]] * (TILE // 128), axis=1)
                buf[at, :] = values
                top_of = jnp.max(values.reshape(chunk // 8, 8, TILE), axis=0)
                highs[m] = top_of if highs[m] is None else jnp.maximum(highs[m], top_of)
            if done is not None:
                powers = jnp.exp((done_buf[at, :] - high[m]) * scale)
                total = jnp.sum(powers.reshape(chunk // 8, 8, TILE), axis=0)
                totals[m] = total if totals[m] is None else totals[m] + total
        if tile is not None:
            for m in range(2):
                top[8 * m : 8 * m + 8, :] = highs[m]
        if done is not None:
            for m in range(2):
                value = high[m] * scale + jnp.log(jnp.sum(totals[m], axis=0, keepdims=True))
                for k in range(TILE // 128):
                    out_ref[m, pl.ds(done * (TILE // 128) + k, 1), :] = value[:, k * 128 : (k + 1) * 128]

    step(0, bufs[0], tops[0], None, None, None)
    for copy in pool_copies[1:]:
        copy.wait()

    def pair(i):
        step(2 * i + 1, bufs[1], tops[1], 2 * i, bufs[0], tops[0])
        step(2 * i + 2, bufs[0], tops[0], 2 * i + 1, bufs[1], tops[1])

    pairs = tiles // 2 - 1
    straight = pairs if pairs <= STRAIGHT else pairs % TOGETHER
    for i in range(straight):
        pair(i)

    def several(j, _):
        for k in range(TOGETHER):
            pair(straight + j * TOGETHER + k)
        return 0

    if pairs > straight:
        lax.fori_loop(0, (pairs - straight) // TOGETHER, several, 0)
    step(tiles - 1, bufs[1], tops[1], tiles - 2, bufs[0], tops[0])
    step(None, None, None, tiles - 1, bufs[1], tops[1])


def partial_kernel(n_pools, n_samples, each, scale, *refs):
    pools, samples, out_ref = refs[:n_pools], refs[n_pools : n_pools + n_samples], refs[n_pools + n_samples]
    joined, half_norm, pool_all, buf0, buf1, top0, top1, sems = refs[n_pools + n_samples + 1 :]
    lse_tiles(pools, samples, each, scale, out_ref, joined, half_norm, pool_all, (buf0, buf1), (top0, top1), sems)


def add_exp(a, b):
    high = jnp.maximum(a, b)
    return high + jnp.log(jnp.exp(a - high) + jnp.exp(b - high))


def last_kernel(n_pools, n_samples, each, scale, place, *refs):
    pools, samples = refs[:n_pools], refs[n_pools : n_pools + n_samples]
    own, beside, swapped, second, third, out_ref, last = refs[n_pools + n_samples : n_pools + n_samples + 7]
    joined, half_norm, pool_all, buf0, buf1, top0, top1, sems = refs[n_pools + n_samples + 7 :]
    lse_tiles(pools, samples, each, scale, last, joined, half_norm, pool_all, (buf0, buf1), (top0, top1), sems)
    y, core = place[0], place[1]
    n = own.shape[1]
    rest = add_exp(second[...], last[:, : 3 * n, :])
    far = add_exp(third[...], last[:, 3 * n :, :])

    def put(owner, value, swapped):
        half = n // 2
        for j in range(4):
            at = lax.rem(owner, 4) * 4 + j
            if swapped:
                out_ref[at, :, pl.ds(core * half, half), :] = value[:, :half, :]
                out_ref[at, :, pl.ds((1 - core) * half, half), :] = value[:, half:, :]
            else:
                out_ref[at, :, :, :] = value

    for i, (owner, part) in enumerate(((y, own), (y + 3 - 2 * core, beside), (y + 1 + 2 * core, swapped))):
        put(owner, add_exp(part[...], rest[:, i * n : (i + 1) * n, :]), False)
    put(y + 2, far, True)


def lse_call(pools, samples, each, scale, earlier=None, place=None):
    count = sum(p.shape[0] for p in pools)
    rows = sum(s.shape[0] for s in samples)
    depth = pools[0].shape[1]
    scratch = [
        pltpu.VMEM((rows, depth), jnp.bfloat16),
        pltpu.VMEM((rows, 128), jnp.float32),
        pltpu.VMEM((count, depth), jnp.bfloat16),
        pltpu.VMEM((rows, TILE), jnp.float32),
        pltpu.VMEM((rows, TILE), jnp.float32),
        pltpu.VMEM((16, TILE), jnp.float32),
        pltpu.VMEM((16, TILE), jnp.float32),
        pltpu.SemaphoreType.DMA((rows // each + len(pools),)),
    ]
    partial = jax.ShapeDtypeStruct((2, count // 128, 128), jnp.float32)
    common = dict(
        out_specs=VMEM,
        compiler_params=pltpu.CompilerParams(vmem_limit_bytes=14 * 1024 * 1024),
        cost_estimate=pl.CostEstimate(
            flops=2 * rows * count * depth, bytes_accessed=2 * (rows + count) * depth, transcendentals=rows * count
        ),
    )
    inputs = [pl.BlockSpec(memory_space=pl.ANY)] * (len(pools) + len(samples))
    if earlier is None:
        kernel = functools.partial(partial_kernel, len(pools), len(samples), each, scale)
        return pl.pallas_call(kernel, out_shape=partial, in_specs=inputs, scratch_shapes=scratch, **common)(*pools, *samples)
    kernel = functools.partial(last_kernel, len(pools), len(samples), each, scale)
    return pl.pallas_call(
        kernel,
        out_shape=jax.ShapeDtypeStruct((16, 2, pools[0].shape[0] // 128, 128), jnp.float32),
        in_specs=[pl.BlockSpec(memory_space=pltpu.SMEM)] + inputs + [VMEM] * len(earlier),
        scratch_shapes=[pltpu.VMEM(partial.shape, jnp.float32)] + scratch,
        **common,
    )(place, *pools, *samples, *earlier)


def merge_kernel(got, norms, ratio_ref, stats_ref):
    value = got[...]
    high = jnp.max(value, axis=0)
    total = high + jnp.log(jnp.sum(jnp.exp(value - high[None]), axis=0))
    log_target = total[0] - norms[...]
    log_ref = total[1] - norms[...]
    ratio = log_target - log_ref
    ratio_ref[...] = ratio
    count = ratio.shape[0] * ratio.shape[1]
    mean = jnp.sum(ratio, axis=(0, 1), keepdims=True) / count
    square = jnp.sum(jnp.square(ratio - mean), axis=(0, 1), keepdims=True) / count
    lane = lax.broadcasted_iota(jnp.int32, stats_ref.shape, 1)
    stats_ref[...] = jnp.where(lane == 0, mean, jnp.where(lane == 1, square, 0.0))


def finish_kernel(ratio, stats, out_ref):
    blocks = stats.shape[0]
    value = stats[...]
    mean = jnp.sum(value[:, 0:1], axis=0, keepdims=True) / blocks
    variance = jnp.sum(value[:, 1:2] + jnp.square(value[:, 0:1] - mean), axis=0, keepdims=True) / blocks
    out_ref[...] = (ratio[...] - mean) / jnp.sqrt(variance + 1e-05)


def swap_core(value):
    return lax.ppermute(value, "core", [(0, 1), (1, 0)])


def swap_x(value):
    return lax.ppermute(value, ("xh", "xl"), [(0, 3), (3, 0), (1, 2), (2, 1)])


def both_ways(value, axis):
    n = SIZES[axis]
    pairs = [(2 * i, 2 * ((i + 1) % n)) for i in range(n)] + [(2 * i + 1, 2 * ((i - 1) % n) + 1) for i in range(n)]
    return lax.ppermute(value, (axis, "core"), pairs)


def body(pool_embeds, target_samples, reference_samples):
    count, depth = pool_embeds.shape
    half = count // 2
    core = lax.axis_index("core")
    each = target_samples.shape[0]
    scale = 2.0 * KERNEL_GAIN / depth
    place = jnp.stack([lax.axis_index("y"), core]).astype(jnp.int32)

    own = jnp.where(
        lax.broadcasted_iota(jnp.int32, (2 * each, depth), 0) < each,
        jnp.pad(target_samples, ((0, each), (0, 0))),
        jnp.pad(reference_samples, ((each, 0), (0, 0))),
    )
    beside = both_ways(pool_embeds, "y")
    other = swap_x(own)
    block = jnp.concatenate([own, swap_core(own)], axis=0)
    z1 = both_ways(block, "z")
    other_block = jnp.concatenate([other, swap_core(other)], axis=0)
    zx1 = both_ways(other_block, "z")
    z2 = both_ways(z1, "z")
    zx2 = both_ways(zx1, "z")
    z3 = both_ways(z2, "z")
    zx3 = both_ways(zx2, "z")
    last = both_ways(jnp.concatenate([z3[: 2 * each], zx3[: 2 * each]], axis=0), "z")
    across = both_ways(lax.dynamic_slice_in_dim(beside, core * half, half, 0), "y")
    swapped = swap_core(beside)
    far = [across, swap_core(across)]
    earliest, early, late = [own, other, z1], [zx1, z2, zx2], [z3, zx3, last]
    parts = []
    for block in (pool_embeds, beside, swapped):
        parts.append(lse_call([block], earliest, each, scale))
    near = [pool_embeds, beside, swapped]
    parts.append(lse_call(near, early, each, scale))
    parts.append(lse_call(far, earliest + early, each, scale))
    send = lse_call(near + far, late, each, scale, parts, place)

    got = lax.all_to_all(send, ROW_GROUP, 0, 0)
    pool_norms = jnp.sum(jnp.square(pool_embeds.astype(jnp.float32)), axis=1) * (KERNEL_GAIN / depth)
    dense = (count // 128, 128)
    blocks = lax.axis_size(BLK)
    log_ratio, stats = pl.pallas_call(
        merge_kernel,
        out_shape=(jax.ShapeDtypeStruct(dense, jnp.float32), jax.ShapeDtypeStruct((blocks, 128), jnp.float32)),
        in_specs=[VMEM, VMEM],
        out_specs=(VMEM, VMEM),
    )(got, pool_norms.reshape(dense))
    stats = lax.all_to_all(stats, BLK, 0, 0, tiled=True)
    standardized = pl.pallas_call(
        finish_kernel, out_shape=jax.ShapeDtypeStruct(dense, jnp.float32), in_specs=[VMEM, VMEM], out_specs=VMEM
    )(log_ratio, stats)
    return (log_ratio.reshape(count), standardized.reshape(count))


def solution(mesh):
    fine = Mesh(mesh.devices.reshape(2, 4, 8, 2, 2), ("xh", "y", "z", "xl", "core"))
    rows = P(BLK, None)
    samples = P(("xh", "y", "z", "xl", "core"), None)
    return jax.shard_map(
        body, mesh=fine, in_specs=(rows, samples, samples), out_specs=(P(BLK), P(BLK)), check_vma=False
    )
```

```python
import functools

import jax
import jax.numpy as jnp
from jax import lax
from jax.experimental import pallas as pl
from jax.experimental.pallas import tpu as pltpu
from jax.sharding import Mesh, PartitionSpec as P


KERNEL_GAIN = 30.0
TILE = 256
CHUNK = 384
STRAIGHT = 5
TOGETHER = 2
SIZES = {"xh": 2, "y": 4, "z": 8, "xl": 2, "core": 2}
ROW_GROUP = ("y", "xl", "core")
BLK = ("xh", "y", "z")
VMEM = pl.BlockSpec(memory_space=pltpu.VMEM)


def lse_tiles(pools, samples, used, each, scale, out_ref, joined, half_norm, pool_all, bufs, tops, sems):
    rows = joined.shape[0]
    member = rows // 2
    sample_copies, pool_copies = [], []
    for ref, taken in zip(samples, used):
        for unit in range(0, taken, 2 * each):
            n = len(sample_copies)
            at = n // 2 * each
            for m in range(2):
                sample_copies.append(
                    pltpu.make_async_copy(
                        ref.at[pl.ds(unit + m * each, each), :], joined.at[pl.ds(at + m * member, each), :], sems.at[n + m]
                    )
                )
    count = 0
    for ref in pools:
        sem = sems.at[len(sample_copies) + len(pool_copies)]
        pool_copies.append(pltpu.make_async_copy(ref, pool_all.at[pl.ds(count, ref.shape[0]), :], sem))
        count += ref.shape[0]
    for copy in sample_copies + pool_copies:
        copy.start()
    for copy in sample_copies:
        copy.wait()

    def norms(i, _):
        at = pl.ds(pl.multiple_of(i * 128, 128), 128)
        wide = joined[at, :].astype(jnp.float32)
        half_norm[at, :] = jnp.broadcast_to(jnp.sum(wide * wide, axis=1, keepdims=True) * 0.5, (128, 128))
        return 0

    lax.fori_loop(0, rows // 128, norms, 0, unroll=True)
    pool_copies[0].wait()
    tiles = count // TILE
    chunk = member // -(-member // CHUNK)

    def step(tile, buf, top, done, done_buf, done_top):
        if tile is not None:
            weights = pool_all[pl.ds(pl.multiple_of(tile * TILE, TILE), TILE), :]
        if done is not None:
            high = [jnp.max(done_top[8 * m : 8 * m + 8, :], axis=0, keepdims=True) for m in range(2)]
        highs, totals = [None, None], [None, None]
        for c in range(rows // chunk):
            m = c * chunk // member
            at = slice(c * chunk, (c + 1) * chunk)
            if tile is not None:
                products = lax.dot_general(
                    joined[at, :], weights, (((1,), (1,)), ((), ())), preferred_element_type=jnp.float32
                )
                values = products - jnp.concatenate([half_norm[at, :]] * (TILE // 128), axis=1)
                buf[at, :] = values
                top_of = jnp.max(values.reshape(chunk // 8, 8, TILE), axis=0)
                highs[m] = top_of if highs[m] is None else jnp.maximum(highs[m], top_of)
            if done is not None:
                powers = jnp.exp((done_buf[at, :] - high[m]) * scale)
                total = jnp.sum(powers.reshape(chunk // 8, 8, TILE), axis=0)
                totals[m] = total if totals[m] is None else totals[m] + total
        if tile is not None:
            for m in range(2):
                top[8 * m : 8 * m + 8, :] = highs[m]
        if done is not None:
            for m in range(2):
                value = high[m] * scale + jnp.log(jnp.sum(totals[m], axis=0, keepdims=True))
                for k in range(TILE // 128):
                    out_ref[m, pl.ds(done * (TILE // 128) + k, 1), :] = value[:, k * 128 : (k + 1) * 128]

    step(0, bufs[0], tops[0], None, None, None)
    for copy in pool_copies[1:]:
        copy.wait()

    def pair(i):
        step(2 * i + 1, bufs[1], tops[1], 2 * i, bufs[0], tops[0])
        step(2 * i + 2, bufs[0], tops[0], 2 * i + 1, bufs[1], tops[1])

    pairs = tiles // 2 - 1
    straight = pairs if pairs <= STRAIGHT else pairs % TOGETHER
    for i in range(straight):
        pair(i)

    def several(j, _):
        for k in range(TOGETHER):
            pair(straight + j * TOGETHER + k)
        return 0

    if pairs > straight:
        lax.fori_loop(0, (pairs - straight) // TOGETHER, several, 0)
    step(tiles - 1, bufs[1], tops[1], tiles - 2, bufs[0], tops[0])
    step(None, None, None, tiles - 1, bufs[1], tops[1])


def partial_kernel(n_pools, n_samples, used, each, scale, *refs):
    pools, samples, out_ref = refs[:n_pools], refs[n_pools : n_pools + n_samples], refs[n_pools + n_samples]
    joined, half_norm, pool_all, buf0, buf1, top0, top1, sems = refs[n_pools + n_samples + 1 :]
    lse_tiles(pools, samples, used, each, scale, out_ref, joined, half_norm, pool_all, (buf0, buf1), (top0, top1), sems)


def add_exp(a, b):
    high = jnp.maximum(a, b)
    return high + jnp.log(jnp.exp(a - high) + jnp.exp(b - high))


def last_kernel(n_pools, n_samples, used, each, scale, *refs):
    pools, samples = refs[:n_pools], refs[n_pools : n_pools + n_samples]
    own, beside, swapped, second, third, out_ref, last = refs[n_pools + n_samples : n_pools + n_samples + 7]
    joined, half_norm, pool_all, buf0, buf1, top0, top1, sems = refs[n_pools + n_samples + 7 :]
    lse_tiles(pools, samples, used, each, scale, last, joined, half_norm, pool_all, (buf0, buf1), (top0, top1), sems)
    y, core = lax.axis_index("y"), lax.axis_index("core")
    n = own.shape[1]
    rest = add_exp(second[...], last[:, : 3 * n, :])
    far = add_exp(third[...], last[:, 3 * n :, :])

    def put(owner, value, swapped):
        half = n // 2
        for j in range(4):
            at = lax.rem(owner, 4) * 4 + j
            if swapped:
                out_ref[at, :, pl.ds(core * half, half), :] = value[:, :half, :]
                out_ref[at, :, pl.ds((1 - core) * half, half), :] = value[:, half:, :]
            else:
                out_ref[at, :, :, :] = value

    for i, (owner, part) in enumerate(((y, own), (y + 3 - 2 * core, beside), (y + 1 + 2 * core, swapped))):
        put(owner, add_exp(part[...], rest[:, i * n : (i + 1) * n, :]), False)
    put(y + 2, far, True)


def lse_call(pools, samples, each, scale, earlier=None, used=None):
    used = used or tuple(s.shape[0] for s in samples)
    count = sum(p.shape[0] for p in pools)
    rows = sum(used)
    depth = pools[0].shape[1]
    scratch = [
        pltpu.VMEM((rows, depth), jnp.bfloat16),
        pltpu.VMEM((rows, 128), jnp.float32),
        pltpu.VMEM((count, depth), jnp.bfloat16),
        pltpu.VMEM((rows, TILE), jnp.float32),
        pltpu.VMEM((rows, TILE), jnp.float32),
        pltpu.VMEM((16, TILE), jnp.float32),
        pltpu.VMEM((16, TILE), jnp.float32),
        pltpu.SemaphoreType.DMA((rows // each + len(pools),)),
    ]
    partial = jax.ShapeDtypeStruct((2, count // 128, 128), jnp.float32)
    common = dict(
        out_specs=VMEM,
        compiler_params=pltpu.CompilerParams(vmem_limit_bytes=14 * 1024 * 1024),
        cost_estimate=pl.CostEstimate(
            flops=2 * rows * count * depth, bytes_accessed=2 * (rows + count) * depth, transcendentals=rows * count
        ),
    )
    inputs = [pl.BlockSpec(memory_space=pl.ANY)] * (len(pools) + len(samples))
    if earlier is None:
        kernel = functools.partial(partial_kernel, len(pools), len(samples), used, each, scale)
        return pl.pallas_call(kernel, out_shape=partial, in_specs=inputs, scratch_shapes=scratch, **common)(*pools, *samples)
    kernel = functools.partial(last_kernel, len(pools), len(samples), used, each, scale)
    return pl.pallas_call(
        kernel,
        out_shape=jax.ShapeDtypeStruct((16, 2, pools[0].shape[0] // 128, 128), jnp.float32),
        in_specs=inputs + [VMEM] * len(earlier),
        scratch_shapes=[pltpu.VMEM(partial.shape, jnp.float32)] + scratch,
        **common,
    )(*pools, *samples, *earlier)


def merge_kernel(norm_scale, got, norms, ratio_ref, stats_ref):
    value = got[...]
    high = jnp.max(value, axis=0)
    total = high + jnp.log(jnp.sum(jnp.exp(value - high[None]), axis=0))
    log_target = total[0] - norms[...] * norm_scale
    log_ref = total[1] - norms[...] * norm_scale
    ratio = log_target - log_ref
    ratio_ref[...] = ratio
    count = ratio.shape[0] * ratio.shape[1]
    mean = jnp.sum(ratio, axis=(0, 1), keepdims=True) / count
    square = jnp.sum(jnp.square(ratio - mean), axis=(0, 1), keepdims=True) / count
    lane = lax.broadcasted_iota(jnp.int32, stats_ref.shape, 1)
    stats_ref[...] = jnp.where(lane == 0, mean, jnp.where(lane == 1, square, 0.0))


def finish_kernel(ratio, stats, out_ref):
    blocks = stats.shape[0]
    value = stats[...]
    mean = jnp.sum(value[:, 0:1], axis=0, keepdims=True) / blocks
    variance = jnp.sum(value[:, 1:2] + jnp.square(value[:, 0:1] - mean), axis=0, keepdims=True) / blocks
    out_ref[...] = (ratio[...] - mean) / jnp.sqrt(variance + 1e-05)


def swap_core(value):
    return lax.ppermute(value, "core", [(0, 1), (1, 0)])


def swap_x(value):
    return lax.ppermute(value, ("xh", "xl"), [(0, 3), (3, 0), (1, 2), (2, 1)])


def both_ways(value, axis):
    n = SIZES[axis]
    pairs = [(2 * i, 2 * ((i + 1) % n)) for i in range(n)] + [(2 * i + 1, 2 * ((i - 1) % n) + 1) for i in range(n)]
    return lax.ppermute(value, (axis, "core"), pairs)


def body(pool_embeds, target_samples, reference_samples):
    count, depth = pool_embeds.shape
    half = count // 2
    core = lax.axis_index("core")
    each = target_samples.shape[0]
    scale = 2.0 * KERNEL_GAIN / depth

    own = jnp.where(
        lax.broadcasted_iota(jnp.int32, (2 * each, depth), 0) < each,
        jnp.pad(target_samples, ((0, each), (0, 0))),
        jnp.pad(reference_samples, ((each, 0), (0, 0))),
    )
    beside = both_ways(pool_embeds, "y")
    pool_norms = jnp.sum(jnp.square(pool_embeds.astype(jnp.float32)), axis=1)
    other = swap_x(own)
    block = jnp.concatenate([own, swap_core(own)], axis=0)
    z1 = both_ways(block, "z")
    other_block = jnp.concatenate([other, swap_core(other)], axis=0)
    zx1 = both_ways(other_block, "z")
    z2 = both_ways(z1, "z")
    zx2 = both_ways(zx1, "z")
    z3 = both_ways(z2, "z")
    zx3 = both_ways(zx2, "z")
    z4, zx4 = both_ways(z3, "z"), both_ways(zx3, "z")
    across = both_ways(lax.dynamic_slice_in_dim(beside, core * half, half, 0), "y")
    swapped = swap_core(beside)
    far = [across, swap_core(across)]
    earliest, early, late = [own, other, z1], [zx1, z2, zx2], [z3, zx3, z4, zx4]
    parts = []
    for block in (pool_embeds, beside, swapped):
        parts.append(lse_call([block], earliest, each, scale))
    near = [pool_embeds, beside, swapped]
    parts.append(lse_call(near, early, each, scale))
    parts.append(lse_call(far, earliest + early, each, scale))
    used = (4 * each, 4 * each, 2 * each, 2 * each)
    send = lse_call(near + far, late, each, scale, parts, used)

    got = lax.all_to_all(send, ROW_GROUP, 0, 0)
    dense = (count // 128, 128)
    blocks = lax.axis_size(BLK)
    log_ratio, stats = pl.pallas_call(
        functools.partial(merge_kernel, KERNEL_GAIN / depth),
        out_shape=(jax.ShapeDtypeStruct(dense, jnp.float32), jax.ShapeDtypeStruct((blocks, 128), jnp.float32)),
        in_specs=[VMEM, VMEM],
        out_specs=(VMEM, VMEM),
    )(got, pool_norms.reshape(dense))
    stats = lax.all_to_all(stats, BLK, 0, 0, tiled=True)
    standardized = pl.pallas_call(
        finish_kernel, out_shape=jax.ShapeDtypeStruct(dense, jnp.float32), in_specs=[VMEM, VMEM], out_specs=VMEM
    )(log_ratio, stats)
    return (log_ratio.reshape(count), standardized.reshape(count))


def solution(mesh):
    fine = Mesh(mesh.devices.reshape(2, 4, 8, 2, 2), ("xh", "y", "z", "xl", "core"))
    rows = P(BLK, None)
    samples = P(("xh", "y", "z", "xl", "core"), None)
    return jax.shard_map(
        body, mesh=fine, in_specs=(rows, samples, samples), out_specs=(P(BLK), P(BLK)), check_vma=False
    )
```

```python
import functools

import jax
import jax.numpy as jnp
from jax import lax
from jax.experimental import pallas as pl
from jax.experimental.pallas import tpu as pltpu
from jax.sharding import Mesh, PartitionSpec as P


KERNEL_GAIN = 30.0
TILE = 256
CHUNK = 384
STRAIGHT = 5
TOGETHER = 2
SIZES = {"xh": 2, "y": 4, "z": 8, "xl": 2, "core": 2}
ROW_GROUP = ("y", "xl", "core")
BLK = ("xh", "y", "z")
VMEM = pl.BlockSpec(memory_space=pltpu.VMEM)


def lse_tiles(pools, samples, used, each, scale, out_ref, joined, half_norm, pool_all, bufs, tops, sems):
    rows = joined.shape[0]
    member = rows // 2
    sample_copies, pool_copies = [], []
    for ref, taken in zip(samples, used):
        for unit in range(0, taken, 2 * each):
            n = len(sample_copies)
            at = n // 2 * each
            for m in range(2):
                sample_copies.append(
                    pltpu.make_async_copy(
                        ref.at[pl.ds(unit + m * each, each), :], joined.at[pl.ds(at + m * member, each), :], sems.at[n + m]
                    )
                )
    count = 0
    for ref in pools:
        sem = sems.at[len(sample_copies) + len(pool_copies)]
        pool_copies.append(pltpu.make_async_copy(ref, pool_all.at[pl.ds(count, ref.shape[0]), :], sem))
        count += ref.shape[0]
    for copy in sample_copies + pool_copies:
        copy.start()
    for copy in sample_copies:
        copy.wait()

    def norms(i, _):
        at = pl.ds(pl.multiple_of(i * 128, 128), 128)
        wide = joined[at, :].astype(jnp.float32)
        half_norm[at, :] = jnp.broadcast_to(jnp.sum(wide * wide, axis=1, keepdims=True) * 0.5, (128, 128))
        return 0

    lax.fori_loop(0, rows // 128, norms, 0, unroll=True)
    pool_copies[0].wait()
    tiles = count // TILE
    chunk = member // -(-member // CHUNK)

    def step(tile, buf, top, done, done_buf, done_top):
        if tile is not None:
            weights = pool_all[pl.ds(pl.multiple_of(tile * TILE, TILE), TILE), :]
        if done is not None:
            high = [jnp.max(done_top[8 * m : 8 * m + 8, :], axis=0, keepdims=True) for m in range(2)]
        highs, totals = [None, None], [None, None]
        for c in range(rows // chunk):
            m = c * chunk // member
            at = slice(c * chunk, (c + 1) * chunk)
            if tile is not None:
                products = lax.dot_general(
                    joined[at, :], weights, (((1,), (1,)), ((), ())), preferred_element_type=jnp.float32
                )
                values = products - jnp.concatenate([half_norm[at, :]] * (TILE // 128), axis=1)
                buf[at, :] = values
                top_of = jnp.max(values.reshape(chunk // 8, 8, TILE), axis=0)
                highs[m] = top_of if highs[m] is None else jnp.maximum(highs[m], top_of)
            if done is not None:
                powers = jnp.exp((done_buf[at, :] - high[m]) * scale)
                total = jnp.sum(powers.reshape(chunk // 8, 8, TILE), axis=0)
                totals[m] = total if totals[m] is None else totals[m] + total
        if tile is not None:
            for m in range(2):
                top[8 * m : 8 * m + 8, :] = highs[m]
        if done is not None:
            for m in range(2):
                value = high[m] * scale + jnp.log(jnp.sum(totals[m], axis=0, keepdims=True))
                for k in range(TILE // 128):
                    out_ref[m, pl.ds(done * (TILE // 128) + k, 1), :] = value[:, k * 128 : (k + 1) * 128]

    step(0, bufs[0], tops[0], None, None, None)
    for copy in pool_copies[1:]:
        copy.wait()

    def pair(i):
        step(2 * i + 1, bufs[1], tops[1], 2 * i, bufs[0], tops[0])
        step(2 * i + 2, bufs[0], tops[0], 2 * i + 1, bufs[1], tops[1])

    pairs = tiles // 2 - 1
    straight = pairs if pairs <= STRAIGHT else pairs % TOGETHER
    for i in range(straight):
        pair(i)

    def several(j, _):
        for k in range(TOGETHER):
            pair(straight + j * TOGETHER + k)
        return 0

    if pairs > straight:
        lax.fori_loop(0, (pairs - straight) // TOGETHER, several, 0)
    step(tiles - 1, bufs[1], tops[1], tiles - 2, bufs[0], tops[0])
    step(None, None, None, tiles - 1, bufs[1], tops[1])


def partial_kernel(n_pools, n_samples, used, each, scale, *refs):
    pools, samples, out_ref = refs[:n_pools], refs[n_pools : n_pools + n_samples], refs[n_pools + n_samples]
    joined, half_norm, pool_all, buf0, buf1, top0, top1, sems = refs[n_pools + n_samples + 1 :]
    lse_tiles(pools, samples, used, each, scale, out_ref, joined, half_norm, pool_all, (buf0, buf1), (top0, top1), sems)


def add_exp(a, b):
    high = jnp.maximum(a, b)
    return high + jnp.log(jnp.exp(a - high) + jnp.exp(b - high))


def last_kernel(n_pools, n_samples, used, each, scale, *refs):
    pools, samples = refs[:n_pools], refs[n_pools : n_pools + n_samples]
    own, beside, swapped, second, third, out_ref, last = refs[n_pools + n_samples : n_pools + n_samples + 7]
    joined, half_norm, pool_all, buf0, buf1, top0, top1, sems = refs[n_pools + n_samples + 7 :]
    lse_tiles(pools, samples, used, each, scale, last, joined, half_norm, pool_all, (buf0, buf1), (top0, top1), sems)
    y, core = lax.axis_index("y"), lax.axis_index("core")
    n = own.shape[1]
    rest = add_exp(second[...], last[:, : 3 * n, :])
    far = add_exp(third[...], last[:, 3 * n :, :])

    def put(owner, value, swapped):
        half = n // 2
        for j in range(4):
            at = lax.rem(owner, 4) * 4 + j
            if swapped:
                out_ref[at, :, pl.ds(core * half, half), :] = value[:, :half, :]
                out_ref[at, :, pl.ds((1 - core) * half, half), :] = value[:, half:, :]
            else:
                out_ref[at, :, :, :] = value

    for i, (owner, part) in enumerate(((y, own), (y + 3 - 2 * core, beside), (y + 1 + 2 * core, swapped))):
        put(owner, add_exp(part[...], rest[:, i * n : (i + 1) * n, :]), False)
    put(y + 2, far, True)


def lse_call(pools, samples, each, scale, earlier=None, used=None):
    used = used or tuple(s.shape[0] for s in samples)
    count = sum(p.shape[0] for p in pools)
    rows = sum(used)
    depth = pools[0].shape[1]
    scratch = [
        pltpu.VMEM((rows, depth), jnp.bfloat16),
        pltpu.VMEM((rows, 128), jnp.float32),
        pltpu.VMEM((count, depth), jnp.bfloat16),
        pltpu.VMEM((rows, TILE), jnp.float32),
        pltpu.VMEM((rows, TILE), jnp.float32),
        pltpu.VMEM((16, TILE), jnp.float32),
        pltpu.VMEM((16, TILE), jnp.float32),
        pltpu.SemaphoreType.DMA((rows // each + len(pools),)),
    ]
    partial = jax.ShapeDtypeStruct((2, count // 128, 128), jnp.float32)
    common = dict(
        out_specs=VMEM,
        compiler_params=pltpu.CompilerParams(vmem_limit_bytes=14 * 1024 * 1024),
        cost_estimate=pl.CostEstimate(
            flops=2 * rows * count * depth, bytes_accessed=2 * (rows + count) * depth, transcendentals=rows * count
        ),
    )
    inputs = [pl.BlockSpec(memory_space=pl.ANY)] * (len(pools) + len(samples))
    if earlier is None:
        kernel = functools.partial(partial_kernel, len(pools), len(samples), used, each, scale)
        return pl.pallas_call(kernel, out_shape=partial, in_specs=inputs, scratch_shapes=scratch, **common)(*pools, *samples)
    kernel = functools.partial(last_kernel, len(pools), len(samples), used, each, scale)
    return pl.pallas_call(
        kernel,
        out_shape=jax.ShapeDtypeStruct((16, 2, pools[0].shape[0] // 128, 128), jnp.float32),
        in_specs=inputs + [VMEM] * len(earlier),
        scratch_shapes=[pltpu.VMEM(partial.shape, jnp.float32)] + scratch,
        **common,
    )(*pools, *samples, *earlier)


def merge_kernel(norm_scale, got, norms, ratio_ref, stats_ref):
    value = got[...]
    high = jnp.max(value, axis=0)
    total = high + jnp.log(jnp.sum(jnp.exp(value - high[None]), axis=0))
    log_target = total[0] - norms[...] * norm_scale
    log_ref = total[1] - norms[...] * norm_scale
    ratio = log_target - log_ref
    ratio_ref[...] = ratio
    count = ratio.shape[0] * ratio.shape[1]
    mean = jnp.sum(ratio, axis=(0, 1), keepdims=True) / count
    square = jnp.sum(jnp.square(ratio - mean), axis=(0, 1), keepdims=True) / count
    lane = lax.broadcasted_iota(jnp.int32, stats_ref.shape, 1)
    stats_ref[...] = jnp.where(lane == 0, mean, jnp.where(lane == 1, square, 0.0))


def finish_kernel(ratio, stats, out_ref):
    blocks = stats.shape[0]
    value = stats[...]
    mean = jnp.sum(value[:, 0:1], axis=0, keepdims=True) / blocks
    variance = jnp.sum(value[:, 1:2] + jnp.square(value[:, 0:1] - mean), axis=0, keepdims=True) / blocks
    out_ref[...] = (ratio[...] - mean) / jnp.sqrt(variance + 1e-05)


def swap_core(value):
    return lax.ppermute(value, "core", [(0, 1), (1, 0)])


def swap_x(value):
    return lax.ppermute(value, ("xh", "xl"), [(0, 3), (3, 0), (1, 2), (2, 1)])


def both_ways(value, axis):
    n = SIZES[axis]
    pairs = [(2 * i, 2 * ((i + 1) % n)) for i in range(n)] + [(2 * i + 1, 2 * ((i - 1) % n) + 1) for i in range(n)]
    return lax.ppermute(value, (axis, "core"), pairs)


def body(pool_embeds, target_samples, reference_samples):
    count, depth = pool_embeds.shape
    half = count // 2
    core = lax.axis_index("core")
    each = target_samples.shape[0]
    scale = 2.0 * KERNEL_GAIN / depth

    own = jnp.where(
        lax.broadcasted_iota(jnp.int32, (2 * each, depth), 0) < each,
        jnp.pad(target_samples, ((0, each), (0, 0))),
        jnp.pad(reference_samples, ((each, 0), (0, 0))),
    )
    beside = both_ways(pool_embeds, "y")
    pool_norms = jnp.sum(jnp.square(pool_embeds.astype(jnp.float32)), axis=1)
    other = swap_x(own)
    block = jnp.concatenate([own, swap_core(own)], axis=0)
    z1 = both_ways(block, "z")
    other_block = jnp.concatenate([other, swap_core(other)], axis=0)
    zx1 = both_ways(other_block, "z")
    z2 = both_ways(z1, "z")
    zx2 = both_ways(zx1, "z")
    z3 = both_ways(z2, "z")
    zx3 = both_ways(zx2, "z")
    z4, zx4 = both_ways(z3[: 2 * each], "z"), both_ways(zx3[: 2 * each], "z")
    across = both_ways(lax.dynamic_slice_in_dim(beside, core * half, half, 0), "y")
    swapped = swap_core(beside)
    far = [across, swap_core(across)]
    earliest, early, late = [own, other, z1], [zx1, z2, zx2], [z3, zx3, z4, zx4]
    parts = []
    for block in (pool_embeds, beside, swapped):
        parts.append(lse_call([block], earliest, each, scale))
    near = [pool_embeds, beside, swapped]
    parts.append(lse_call(near, early, each, scale))
    parts.append(lse_call(far, earliest + early, each, scale))
    send = lse_call(near + far, late, each, scale, parts)

    got = lax.all_to_all(send, ROW_GROUP, 0, 0)
    dense = (count // 128, 128)
    blocks = lax.axis_size(BLK)
    log_ratio, stats = pl.pallas_call(
        functools.partial(merge_kernel, KERNEL_GAIN / depth),
        out_shape=(jax.ShapeDtypeStruct(dense, jnp.float32), jax.ShapeDtypeStruct((blocks, 128), jnp.float32)),
        in_specs=[VMEM, VMEM],
        out_specs=(VMEM, VMEM),
    )(got, pool_norms.reshape(dense))
    stats = lax.all_to_all(stats, BLK, 0, 0, tiled=True)
    standardized = pl.pallas_call(
        finish_kernel, out_shape=jax.ShapeDtypeStruct(dense, jnp.float32), in_specs=[VMEM, VMEM], out_specs=VMEM
    )(log_ratio, stats)
    return (log_ratio.reshape(count), standardized.reshape(count))


def solution(mesh):
    fine = Mesh(mesh.devices.reshape(2, 4, 8, 2, 2), ("xh", "y", "z", "xl", "core"))
    rows = P(BLK, None)
    samples = P(("xh", "y", "z", "xl", "core"), None)
    return jax.shard_map(
        body, mesh=fine, in_specs=(rows, samples, samples), out_specs=(P(BLK), P(BLK)), check_vma=False
    )
```
